128 devices in a mesh: gx: 8 (over y, core), gy: 16 (over x, z).
Axes of the slice: x: 4, y: 4, z: 4, core: 2. Of those that a mesh axis runs over, the one named last changes fastest.
Arguments:
- cotangent: float32 [6, 8, 1024, 1024], P(None, None, 'gy', 'gx'), may hold values from -6 to 6
- permeability: float32 [6, 1024, 1024], P(None, 'gy', 'gx'), may hold values from 0.2 to 5
- well_mask: int32 [1024, 1024], P('gy', 'gx'), may hold values 0 or 1
- diag_block: bfloat16 [6, 8, 8, 1024, 1024], P(None, None, None, 'gy', 'gx'), may hold values from -2 to 2
- flux_block: bfloat16 [6, 8, 8, 1024, 1024], P(None, None, None, 'gy', 'gx'), may hold values from -0.875 to 0.875
- cell_list: int32 [16, 8, 16384], P('gy', 'gx'), may hold values from 0 to 49151, as said below
- block_count: int32 [16, 8], P('gy', 'gx'), may hold values from 64 to 128, as said below
- helper_of: int32 [16, 8, 128], P('gy', 'gx'), may hold values from 0 to 127, as said below
- flash_inverse: bfloat16 [16, 8, 128, 8, 8, 128], P('gy', 'gx'), may hold values from -2 to 2
- flash_coupling: bfloat16 [16, 8, 128, 8, 8, 128], P('gy', 'gx'), may hold values from -2 to 2
- phase_state: bfloat16 [16, 8, 128, 8, 128], P('gy', 'gx'), may hold values from 0.049804688 to 1
Outputs:
- adjoint: float32 [6, 8, 1024, 1024], P(None, None, 'gy', 'gx')
- interaction_grad: float32 [8, 8], replicated
The draws below stay inside these ranges and needn't reach their ends.
Inputs may be any that keep to these rules, and one draw needn't show every extreme that they name: `cell_list`: within one brick the 16384 entries are distinct cells of that brick. `block_count`: some brick has 128 live blocks. `helper_of`: each brick's row is a permutation of all helpers; helper h is the device at gx index h // 16 and gy index h % 16.
All inputs are finite; a program needn't handle non-finite values. No bound on the sum of `well_mask` on one device may be relied on, other than what follows from the above.
Results may differ from the reference program's by a relative error of at most 0.0075.
Values may be sent and summed in bfloat16 or wider, within the bound.
A program may use at most 192 MiB of HBM per device.

```python
import math
import jax
import jax.numpy as jnp
from jax import lax

NC = 8
BLK = 128
LAYERS = 6
CY = 64
CX = 128
NY = 1024
NX = 1024
BRICKS_Y = 16
BRICKS_X = 8
BLK_MOST = 128
SLOTS = 16384
CELLS = 49152


def draw_cell_list(key, part):
    brick_keys = jax.random.split(jax.random.fold_in(key, 11), BRICKS_Y * BRICKS_X)

    def one_brick(brick_key):
        return jax.random.permutation(brick_key, LAYERS * CY * CX)[:SLOTS].astype(jnp.int32)
    return jax.vmap(one_brick)(brick_keys).reshape(BRICKS_Y, BRICKS_X, SLOTS)


def draw_block_count(key, part):
    count_key = jax.random.fold_in(key, 23)
    first_key, second_key = jax.random.split(count_key)
    counts = jax.random.randint(first_key, (BRICKS_Y * BRICKS_X,), BLK_MOST // 2, BLK_MOST + 1)
    chosen = jax.random.randint(second_key, (), 0, BRICKS_Y * BRICKS_X)
    counts = counts.at[chosen].set(BLK_MOST)
    return counts.reshape(BRICKS_Y, BRICKS_X).astype(jnp.int32)


def draw_helper_of(key, part):
    brick_keys = jax.random.split(jax.random.fold_in(key, 37), BRICKS_Y * BRICKS_X)

    def one_brick(brick_key):
        return jax.random.permutation(brick_key, BLK_MOST).astype(jnp.int32)
    return jax.vmap(one_brick)(brick_keys).reshape(BRICKS_Y, BRICKS_X, BLK_MOST)


def plant(values, own_key, low, high):
    longest = values.shape.index(max(values.shape))
    spots = []
    for shift in (0, 1):
        where = [jax.random.randint(jax.random.fold_in(own_key, axis), (), 0, length) for axis, length in enumerate(values.shape)]
        where[longest] = (where[longest] + shift) % values.shape[longest]
        spots.append(tuple(where))
    return values.at[spots[0]].set(low).at[spots[1]].set(high)


def levels(key, extent, cuts, low, largest):
    loudness, own = 1.0, jax.random.fold_in(key, 6)
    for position, parts in cuts:
        heights = jnp.exp(jax.random.uniform(jax.random.fold_in(own, position), (parts,), jnp.float32, low / len(cuts), largest / len(cuts)))
        loudness = loudness * jnp.repeat(heights, extent[position] // parts).reshape([-1 if axis == position else 1 for axis in range(len(extent))])
    return loudness


def gaussian(own_key, shape, deviation, limit, pieces=(), held_as=jnp.bfloat16):
    values = jax.random.normal(own_key, shape, jnp.float32) * deviation
    if len(pieces) > 0:
        values = levels(own_key, shape, pieces, -0.22, 0.18) * values
    return jnp.clip(values, min=-limit, max=limit).astype(held_as)


def setup_inputs(seed: int = 0) -> dict:
    key_of = jax.random.split(jax.random.key(seed), 12)
    cotangent = gaussian(key_of[0], (LAYERS, NC, NY, NX), 1.0, 6.0, ((2, 16), (3, 8)), jnp.float32)
    permeability = jnp.clip(jnp.exp(math.log(5.0) - 3.218876 * jax.random.uniform(key_of[1], (LAYERS, NY, NX), jnp.float32) ** levels(key_of[1], (LAYERS, NY, NX), ((1, 16), (2, 8)), -0.2, 0.2)), 0.2, 5.0)
    well_mask = plant((jax.random.randint(key_of[2], (NY, NX), 0, 16) < 1).astype(jnp.int32), jax.random.fold_in(key_of[2], 1), 0, 1)
    diag_block = gaussian(key_of[3], (LAYERS, NC, NC, NY, NX), NC ** -0.5, 2.0, ((3, 16), (4, 8)))
    flux_block = gaussian(key_of[4], (LAYERS, NC, NC, NY, NX), (6 * NC) ** -0.5, 0.875, ((3, 16), (4, 8)))
    cell_list = draw_cell_list(jax.random.fold_in(key_of[11], 71), 0)
    block_count = draw_block_count(jax.random.fold_in(key_of[11], 71), 0)
    helper_of = draw_helper_of(jax.random.fold_in(key_of[11], 71), 0)
    flash_inverse = gaussian(key_of[8], (BRICKS_Y, BRICKS_X, BLK_MOST, NC, NC, BLK), NC ** -0.5, 2.0, ((0, 16), (1, 8)))
    flash_coupling = gaussian(key_of[9], (BRICKS_Y, BRICKS_X, BLK_MOST, NC, NC, BLK), NC ** -0.5, 2.0, ((0, 16), (1, 8)))
    phase_state = jnp.clip(0.049804688 + 0.9501953 * jax.random.uniform(key_of[10], (BRICKS_Y, BRICKS_X, BLK_MOST, NC, BLK), jnp.float32) ** levels(key_of[10], (BRICKS_Y, BRICKS_X, BLK_MOST, NC, BLK), ((0, 16), (1, 8)), -0.2, 0.2), 0.049804688, 1.0).astype(jnp.bfloat16)
    return dict(cotangent=cotangent, permeability=permeability, well_mask=well_mask, diag_block=diag_block, flux_block=flux_block, cell_list=cell_list, block_count=block_count, helper_of=helper_of, flash_inverse=flash_inverse, flash_coupling=flash_coupling, phase_state=phase_state)


OFFSETS = ((1, 0, 0), (-1, 0, 0), (0, 1, 0), (0, -1, 0), (0, 0, 1), (0, 0, -1))

def transmissibility(padded_perm, layers, rows_y, cols_x):
    centre = padded_perm[1:1 + layers, 1:1 + rows_y, 1:1 + cols_x]
    result = []
    for step_z, step_y, step_x in OFFSETS:
        beside = padded_perm[1 + step_z:1 + step_z + layers, 1 + step_y:1 + step_y + rows_y, 1 + step_x:1 + step_x + cols_x]
        result.append(2.0 * centre * beside / (centre + beside))
    return result

def neighbour_sum(padded, trans_list, layers, rows_y, cols_x):
    summed = jnp.zeros((layers, padded.shape[1], rows_y, cols_x), jnp.float32)
    for weights, (step_z, step_y, step_x) in zip(trans_list, OFFSETS):
        beside = padded[1 + step_z:1 + step_z + layers, :, 1 + step_y:1 + step_y + rows_y, 1 + step_x:1 + step_x + cols_x]
        summed = summed + weights[:, None] * beside
    return summed

def blocks_transposed(blocks, source_field):

    def layer_term(layer_pair):
        return lax.optimization_barrier(jnp.sum(layer_pair[0].astype(jnp.float32) * layer_pair[1][:, None], axis=0))
    return lax.map(layer_term, (blocks, source_field))

def apply_transposed(source_field, well_field, trans_list, diag_block, flux_block):
    layers, components, rows_y, cols_x = source_field.shape
    masked = source_field * (1.0 - well_field)
    padded = jnp.pad(masked, ((1, 1), (0, 0), (1, 1), (1, 1)))
    summed = neighbour_sum(padded, trans_list, layers, rows_y, cols_x)
    return blocks_transposed(diag_block, masked) - blocks_transposed(flux_block, summed) + well_field * source_field

def flash_terms(inverse, coupling, chosen, phase_rows):
    multiplier = jnp.einsum('nrck,nrk->nck', inverse.astype(jnp.float32), chosen.astype(jnp.float32))
    correction = (-jnp.einsum('nrck,nrk->nck', coupling.astype(jnp.float32), multiplier)).astype(jnp.bfloat16)
    state_wide = phase_rows.astype(jnp.float32)
    partial_sum = jnp.einsum('nik,njk->ij', multiplier * state_wide, state_wide)
    return (correction, partial_sum)

def reference(cotangent, permeability, well_mask, diag_block, flux_block, cell_list, block_count, helper_of, flash_inverse, flash_coupling, phase_state):
    well_field = well_mask.astype(jnp.float32)
    layers, components, total_y, total_x = cotangent.shape
    trans_list = transmissibility(jnp.pad(permeability, 1), layers, total_y, total_x)
    first_apply = apply_transposed(cotangent, well_field, trans_list, diag_block, flux_block)
    bricks = first_apply.reshape(layers, components, BRICKS_Y, CY, BRICKS_X, CX).transpose(2, 4, 1, 0, 3, 5).reshape(BRICKS_Y, BRICKS_X, components, CELLS)
    gather_index = jnp.broadcast_to(cell_list[:, :, None, :], (BRICKS_Y, BRICKS_X, components, SLOTS))
    picked = jnp.take_along_axis(bricks, gather_index, axis=3)
    picked = picked.reshape(BRICKS_Y, BRICKS_X, components, BLK_MOST, BLK).transpose(0, 1, 3, 2, 4)
    live_slots = jnp.arange(BLK_MOST, dtype=jnp.int32)[None, None, :] < block_count[:, :, None]
    picked = jnp.where(live_slots[:, :, :, None, None], picked, 0.0).astype(jnp.bfloat16)
    brick_y = jnp.arange(BRICKS_Y, dtype=jnp.int32)[:, None, None]
    brick_x = jnp.arange(BRICKS_X, dtype=jnp.int32)[None, :, None]
    source = jnp.broadcast_to(brick_x * BRICKS_Y + brick_y, (BRICKS_Y, BRICKS_X, BLK_MOST)).astype(jnp.int32)
    helper_y = (helper_of % BRICKS_Y).astype(jnp.int32)
    helper_x = (helper_of // BRICKS_Y).astype(jnp.int32)
    at_helper = jnp.zeros((BRICKS_Y, BRICKS_X, BLK_MOST, components, BLK), jnp.bfloat16).at[helper_y, helper_x, source].set(picked)

    def helper_row(row_group):
        inverse, coupling, chosen, phase_rows = row_group
        correction, partial_sum = flash_terms(inverse.reshape(-1, components, components, BLK), coupling.reshape(-1, components, components, BLK), chosen.reshape(-1, components, BLK), phase_rows.reshape(-1, components, BLK))
        return (correction.reshape(BRICKS_X, BLK_MOST, components, BLK), partial_sum)
    corrections_h, partials = lax.map(helper_row, (flash_inverse, flash_coupling, at_helper, phase_state))
    grad_scale = 1.0 / math.sqrt(BLK * BLK_MOST * BLK_MOST)
    interaction_grad = -grad_scale * lax.optimization_barrier(jnp.sum(partials, axis=0))
    corrections = corrections_h[helper_y, helper_x, source]
    values = corrections.transpose(0, 1, 3, 2, 4).reshape(BRICKS_Y, BRICKS_X, components, SLOTS).astype(jnp.float32)

    def add_cells(cells_row, where_cells, amount):
        return cells_row.at[:, where_cells].add(amount)
    updated = jax.vmap(jax.vmap(add_cells))(bricks, cell_list, values)
    second = updated.reshape(BRICKS_Y, BRICKS_X, components, layers, CY, CX).transpose(3, 2, 0, 4, 1, 5).reshape(layers, components, total_y, total_x)
    adjoint = apply_transposed(second, well_field, trans_list, diag_block, flux_block)
    return (adjoint, interaction_grad)
```

```python
import functools
import math

import jax
import jax.numpy as jnp
from jax import lax
from jax.experimental import pallas as pl
from jax.experimental.pallas import tpu as pltpu
from jax.sharding import PartitionSpec as P

MESH = pl.DeviceIdType.MESH
F32 = jnp.float32
BF16 = jnp.bfloat16

LAYERS, NC, CY, CX = 6, 8, 64, 128
FIELDS = LAYERS * NC
PAD = 80
WX, WY = 8, 16
DEVICES = WX * WY
BLOCKS, BLK = 128, 128
NB = 8
CHUNKS = BLOCKS // NB
DELAY = 5
ROWS = 16


def kernel(
    cot_h, perm_h, mask_h, diag_h, flux_h, cells_ref, count_ref, helper_ref, inv_h, coup_h, phase_h,
    out_h, grad_ref,
    cot_v, perm_v, mask_v, diag_v, flux_v, inv_v, coup_v, phase_v,
    w_v, k_v, t_v, f16_v, s2_v, code_v, y_v, oh_v, lhs_v,
    ps, rb, cs, cr, g_v, gt, ga, gt2, gb,
    hx_s, hx_r, hy_s, hy_r, out_v,
    load_sem, blk_sem, fl_sem, out_sem,
    halo_send, halo_recv, ps_send, ps_recv, cs_send, cs_recv, g_send, g_recv,
):
    gx = lax.axis_index("gx")
    gy = lax.axis_index("gy")
    me = gx * WY + gy

    def device(linear):
        return (lax.div(linear, WY), lax.rem(linear, WY))

    loads = [
        pltpu.make_async_copy(cot_h, cot_v, load_sem.at[0]),
        pltpu.make_async_copy(perm_h, perm_v, load_sem.at[1]),
        pltpu.make_async_copy(mask_h, mask_v, load_sem.at[2]),
    ]
    for copy in loads:
        copy.start()

    def block_copies(layer):
        return (
            pltpu.make_async_copy(diag_h.at[layer], diag_v.at[layer], blk_sem.at[0, layer]),
            pltpu.make_async_copy(flux_h.at[layer], flux_v.at[layer], blk_sem.at[1, layer]),
        )

    for layer in range(LAYERS):
        for copy in block_copies(layer):
            copy.start()
    flash_loads = [
        pltpu.make_async_copy(inv_h, inv_v, fl_sem.at[0]),
        pltpu.make_async_copy(coup_h, coup_v, fl_sem.at[1]),
        pltpu.make_async_copy(phase_h, phase_v, fl_sem.at[2]),
    ]
    for copy in flash_loads:
        copy.start()

    barrier = pltpu.get_barrier_semaphore()

    def greet(step, carry):
        pl.semaphore_signal(
            barrier, inc=1, device_id=device(lax.rem(me + step, DEVICES)), device_id_type=MESH
        )
        return carry

    lax.fori_loop(1, DEVICES, greet, 0)

    lane_i = lax.broadcasted_iota(jnp.int32, (BLOCKS, BLK), 1)
    row_i = lax.broadcasted_iota(jnp.int32, (BLOCKS, BLK), 0)
    target = lax.rem(row_i + me, DEVICES)
    choose = jnp.where(helper_ref[...] == target, 1.0, 0.0).astype(BF16)
    cells = cells_ref[...]
    cell_layer = lax.shift_right_logical(cells, 13).astype(F32).astype(BF16)
    cell_y = lax.shift_right_logical(cells, 7) & (CY - 1)
    cell_y = jnp.where(row_i < count_ref[0, 0], cell_y, CY).astype(F32).astype(BF16)
    cell_x = (cells & (CX - 1)).astype(F32).astype(BF16)
    code_v[...] = CX * jnp.dot(choose, cell_layer, preferred_element_type=F32) + jnp.dot(
        choose, cell_x, preferred_element_type=F32
    )
    y_v[...] = jnp.dot(choose, cell_y, preferred_element_type=F32)

    w_v[pl.ds(0, NC * PAD), :] = jnp.zeros((NC * PAD, CX), F32)
    w_v[pl.ds((FIELDS + NC) * PAD, NC * PAD), :] = jnp.zeros((NC * PAD, CX), F32)
    k_v[pl.ds(0, PAD), :] = jnp.zeros((PAD, CX), F32)
    k_v[pl.ds((LAYERS + 1) * PAD, PAD), :] = jnp.zeros((PAD, CX), F32)

    for copy in loads:
        copy.wait()

    lane_y = lax.broadcasted_iota(jnp.int32, (CY, CX), 1)
    hole = mask_v[...].astype(F32)
    keep = 1.0 - hole

    def field(q):
        return pl.ds(pl.multiple_of(q * CY, CY), CY)

    def pack_edges(q, value, carry):
        right, left = carry
        turned = pltpu.roll(value, 2 * q + 2, axis=1)
        right = jnp.where(lane_y == 2 * q + 1, turned, right)
        left = jnp.where(lane_y == 2 * q + 2, turned, left)
        return right, left

    def mask_fields(source, which, start):
        def step(q, carry):
            value = source[field(q), :] * keep
            w_v[pl.ds(pl.multiple_of((q + NC) * PAD + 8, 8), CY), :] = value
            return pack_edges(q, value, carry)

        right, left = lax.fori_loop(0, FIELDS, step, start, unroll=2)
        hx_s[which, 0] = left
        hx_s[which, 1] = right
        for layer in range(LAYERS):
            base = (layer + 1) * NC * PAD + 8
            hy_s[which, 0, pl.ds(layer * NC, NC), :] = w_v[pl.ds(base, NC, stride=PAD), :]
            hy_s[which, 1, pl.ds(layer * NC, NC), :] = w_v[pl.ds(base + CY - 1, NC, stride=PAD), :]

    def halo_copies(which):
        east = (lax.rem(gx + 1, WX), gy)
        west = (lax.rem(gx + WX - 1, WX), gy)
        south = (gx, lax.rem(gy + 1, WY))
        north = (gx, lax.rem(gy + WY - 1, WY))
        plan = (
            (hx_s.at[which, 1], hx_r.at[which, 0], east),
            (hx_s.at[which, 0], hx_r.at[which, 1], west),
            (hy_s.at[which, 1], hy_r.at[which, 0], south),
            (hy_s.at[which, 0], hy_r.at[which, 1], north),
        )
        return [
            pltpu.make_async_remote_copy(
                src_ref=source,
                dst_ref=target_ref,
                send_sem=halo_send.at[which, i],
                recv_sem=halo_recv.at[which, i],
                device_id=where,
                device_id_type=MESH,
            )
            for i, (source, target_ref, where) in enumerate(plan)
        ]

    def edge_columns(which):
        odd = lax.rem(lane_y, 2) == 1
        from_west = jnp.where(gx > 0, hx_r[which, 0], 0.0)
        from_east = jnp.where(gx < WX - 1, hx_r[which, 1], 0.0)
        hx_r[which, 0] = jnp.where(odd, from_west, from_east)

    def edge_rows(which):
        for layer in range(LAYERS):
            base = (layer + 1) * NC * PAD
            rows = pl.ds(layer * NC, NC)
            w_v[pl.ds(base + 7, NC, stride=PAD), :] = jnp.where(gy > 0, hy_r[which, 0, rows, :], 0.0)
            w_v[pl.ds(base + 8 + CY, NC, stride=PAD), :] = jnp.where(
                gy < WY - 1, hy_r[which, 1, rows, :], 0.0
            )

    zero_edge = jnp.zeros((CY, CX), F32)
    start = (zero_edge, zero_edge)
    for layer in range(LAYERS):
        value = perm_v[pl.ds(layer * CY, CY), :]
        k_v[pl.ds((layer + 1) * PAD + 8, CY), :] = value
        start = pack_edges(FIELDS + layer, value, start)
    mask_fields(cot_v, 0, start)
    for layer in range(LAYERS):
        base = (layer + 1) * PAD + 8
        hy_s[0, 0, pl.ds(FIELDS + layer, 1), :] = k_v[pl.ds(base, 1), :]
        hy_s[0, 1, pl.ds(FIELDS + layer, 1), :] = k_v[pl.ds(base + CY - 1, 1), :]

    pl.semaphore_wait(barrier, DEVICES - 1)
    first_halo = halo_copies(0)
    for copy in first_halo:
        copy.start()
    for copy in first_halo:
        copy.wait_recv()

    edge_columns(0)
    edge_rows(0)
    for layer in range(LAYERS):
        base = (layer + 1) * PAD
        k_v[pl.ds(base + 7, 1), :] = jnp.where(gy > 0, hy_r[0, 0, pl.ds(FIELDS + layer, 1), :], 0.0)
        k_v[pl.ds(base + 8 + CY, 1), :] = jnp.where(
            gy < WY - 1, hy_r[0, 1, pl.ds(FIELDS + layer, 1), :], 0.0
        )

    def beside_x(value, edges, shift, lane):
        turned = pltpu.roll(edges, shift, axis=1)
        west = pltpu.roll(jnp.where(lane == CX - 1, turned, value), 1, axis=1)
        east = pltpu.roll(jnp.where(lane == 0, turned, value), CX - 1, axis=1)
        return west, east

    def make_weights(layer, carry):
        base = pl.multiple_of((layer + 1) * PAD, 8)
        centre = k_v[pl.ds(base + 8, CY), :]
        west, east = beside_x(centre, hx_r[0, 0], CX - 2 * (FIELDS + layer) - 2, lane_y)
        others = (
            k_v[pl.ds(base + 8 + PAD, CY), :],
            k_v[pl.ds(base + 8 - PAD, CY), :],
            k_v[pl.ds(base + 9, CY), :],
            k_v[pl.ds(base + 7, CY), :],
            east,
            west,
        )
        for i, other in enumerate(others):
            t_v[i, field(layer), :] = 2.0 * centre * other / (centre + other)
        return carry

    lax.fori_loop(0, LAYERS, make_weights, 0)

    lane_r = lax.broadcasted_iota(jnp.int32, (ROWS, CX), 1)

    def blocks(layer, which, source, put):
        for part in range(CY // ROWS):
            r0 = part * ROWS
            rows = pl.ds(pl.multiple_of(layer * CY + r0, ROWS), ROWS)
            weights = [t_v[i, rows, :] for i in range(6)]
            edges = hx_r[which, 0, pl.ds(r0, ROWS), :]
            own, around = [], []
            for c in range(NC):
                base = pl.multiple_of((layer + 1) * (NC * PAD) + (c * PAD + 8 + r0), 8)
                value = w_v[pl.ds(base, ROWS), :]
                shift = CX - 2 * (layer * NC + c) - 2
                west, east = beside_x(value, edges, shift, lane_r)
                total = weights[0] * w_v[pl.ds(base + NC * PAD, ROWS), :]
                total = total + weights[1] * w_v[pl.ds(base - NC * PAD, ROWS), :]
                total = total + weights[2] * w_v[pl.ds(base + 1, ROWS), :]
                total = total + weights[3] * w_v[pl.ds(base - 1, ROWS), :]
                total = total + weights[4] * east
                total = total + weights[5] * west
                own.append(value)
                around.append(total)
            well = mask_v[pl.ds(r0, ROWS), :].astype(F32)
            for c in range(NC):
                frm = pl.ds(pl.multiple_of((layer * NC + c) * CY + r0, ROWS), ROWS)
                acc = well * source[frm, :]
                for r in range(NC):
                    acc = acc + diag_v[layer, r, c, pl.ds(r0, ROWS), :].astype(F32) * own[r]
                    acc = acc - flux_v[layer, r, c, pl.ds(r0, ROWS), :].astype(F32) * around[r]
                put(layer, c, r0, acc)

    def put_first(layer, c, r0, value):
        lanes = pl.ds(pl.multiple_of(layer * CX, CX), CX)
        f16_v[pl.ds(c * CY + r0, ROWS), lanes] = value.astype(BF16)
        s2_v[pl.ds(pl.multiple_of((layer * NC + c) * CY + r0, ROWS), ROWS), :] = value

    def first_layer(layer, carry):
        for copy in block_copies(layer):
            copy.wait()
        blocks(layer, 0, cot_v, put_first)
        return carry

    lax.fori_loop(0, LAYERS, first_layer, 0)
    for copy in flash_loads:
        copy.wait()

    iota_x = lax.broadcasted_iota(jnp.int32, (CX, BLK), 0).astype(F32).astype(BF16)
    iota_y = lax.broadcasted_iota(jnp.int32, (CY, BLK), 0).astype(F32)
    one16 = jnp.ones((CX, BLK), BF16)
    zero16 = jnp.zeros((CX, BLK), BF16)

    def one_hot(p, b):
        code = code_v[pl.ds(p, 1), :]
        for layer in range(LAYERS):
            own_x = jnp.broadcast_to((code - float(layer * CX)).astype(BF16), (CX, BLK))
            oh_v[pl.ds(layer * CX, CX), pl.ds(b * BLK, BLK)] = jnp.where(own_x == iota_x, one16, zero16)

    def send_block(buf, to, p, peer, send, recv, chunk):
        return pltpu.make_async_remote_copy(
            src_ref=buf.at[p],
            dst_ref=to.at[p],
            send_sem=send.at[chunk],
            recv_sem=recv.at[chunk],
            device_id=device(peer),
            device_id_type=MESH,
        )

    def chunk_copy(buf, to, chunk, first, send, recv):
        rows = pl.ds(chunk * NB + first, NB - first)
        return pltpu.make_async_remote_copy(
            src_ref=buf.at[rows],
            dst_ref=to.at[rows],
            send_sem=send.at[chunk],
            recv_sem=recv.at[chunk],
            device_id=device(lax.rem(me + 1, DEVICES)),
            device_id_type=MESH,
        )

    def wait_chunk(buf, to, chunk, send, recv, sent):
        for first in (1, 0):
            @pl.when((chunk == 0) if first else (chunk > 0))
            def _():
                copy = chunk_copy(buf, to, chunk, first, send, recv)
                if sent:
                    copy.wait_send()
                else:
                    copy.wait_recv()

    def gather(chunk):
        for b in range(NB):
            one_hot(chunk * NB + b, b)
        wide = jnp.dot(f16_v[...], oh_v[...], preferred_element_type=F32)
        for b in range(NB):
            p = chunk * NB + b
            hit = jnp.broadcast_to(y_v[pl.ds(p, 1), :], (CY, BLK)) == iota_y
            found = []
            for c in range(NC):
                piece = wide[c * CY : (c + 1) * CY, b * BLK : (b + 1) * BLK]
                found.append(jnp.sum(jnp.where(hit, piece, 0.0), axis=0, keepdims=True))
            picked = jnp.concatenate(found, axis=0).astype(BF16)
            ps[p] = picked
            if b == 0:
                @pl.when(chunk == 0)
                def _():
                    rb[p] = picked

                @pl.when(chunk > 0)
                def _():
                    send_block(ps, rb, p, lax.rem(me + p, DEVICES), ps_send, ps_recv, chunk).start()
            else:
                send_block(ps, rb, p, lax.rem(me + p, DEVICES), ps_send, ps_recv, chunk).start()

    def flash(chunk):
        wait_chunk(ps, rb, chunk, ps_send, ps_recv, False)
        for b in range(NB):
            p = chunk * NB + b
            source = lax.rem(me - p + DEVICES, DEVICES)
            chosen = rb[p].astype(F32)
            multiplier = jnp.sum(inv_v[source].astype(F32) * chosen[:, None, :], axis=0)
            change = -jnp.sum(coup_v[source].astype(F32) * multiplier[:, None, :], axis=0)
            state = phase_v[source].astype(F32)
            g_v[...] += (multiplier * state)[None] * state[:, None, :]
            change = change.astype(BF16)
            cs[p] = change
            if b == 0:
                @pl.when(chunk == 0)
                def _():
                    cr[p] = change

                @pl.when(chunk > 0)
                def _():
                    send_block(cs, cr, p, source, cs_send, cs_recv, chunk).start()
            else:
                send_block(cs, cr, p, source, cs_send, cs_recv, chunk).start()

    def scatter(chunk):
        wait_chunk(cs, cr, chunk, cs_send, cs_recv, False)
        for b in range(NB):
            p = chunk * NB + b
            one_hot(p, b)
            hit = jnp.broadcast_to(y_v[pl.ds(p, 1), :], (CY, BLK)) == iota_y
            change = cr[p].astype(F32)
            for c in range(NC):
                lhs_v[pl.ds(c * CY, CY), pl.ds(b * BLK, BLK)] = jnp.where(
                    hit, jnp.broadcast_to(change[c : c + 1], (CY, BLK)), 0.0
                ).astype(BF16)
        added = lax.dot_general(
            lhs_v[...], oh_v[...], (((1,), (1,)), ((), ())), preferred_element_type=F32
        )
        for layer in range(LAYERS):
            rows = pl.ds(layer * NC * CY, NC * CY)
            s2_v[rows, :] = s2_v[rows, :] + added[:, layer * CX : (layer + 1) * CX]

    g_v[...] = jnp.zeros_like(g_v)

    def loop(low, high, *steps):
        def body(t, carry):
            for step, back in steps:
                step(t - back)
            return carry

        lax.fori_loop(low, high, body, 0)

    loop(0, DELAY, (gather, 0))
    loop(DELAY, CHUNKS, (gather, 0), (flash, DELAY))
    loop(CHUNKS, CHUNKS + DELAY, (flash, DELAY), (scatter, CHUNKS))

    lane_g = lax.broadcasted_iota(jnp.int32, (NC, CX), 1)
    tile = jnp.zeros((NC, CX), F32)
    for j in range(NC):
        tile = jnp.where(lane_g == j, jnp.sum(g_v[j], axis=1, keepdims=True), tile)
    gt[...] = tile
    ga[gx] = tile

    def grad_copy(source, target_ref, where, phase):
        return pltpu.make_async_remote_copy(
            src_ref=source,
            dst_ref=target_ref,
            send_sem=g_send.at[phase],
            recv_sem=g_recv.at[phase],
            device_id=where,
            device_id_type=MESH,
        )

    def send_x(step, carry):
        grad_copy(gt, ga.at[gx], (lax.rem(gx + step, WX), gy), 0).start()
        return carry

    lax.fori_loop(1, WX, send_x, 0)

    loop(CHUNKS + DELAY, 2 * CHUNKS, (scatter, CHUNKS))

    some = ga.at[pl.ds(0, WX - 1)]
    grad_copy(some, some, (lax.rem(gx + 1, WX), gy), 0).wait_recv()
    part = ga[0]
    for i in range(1, WX):
        part = part + ga[i]
    gt2[...] = part
    gb[gy] = part

    def send_y(step, carry):
        grad_copy(gt2, gb.at[gy], (gx, lax.rem(gy + step, WY)), 1).start()
        return carry

    lax.fori_loop(1, WY, send_y, 0)

    mask_fields(s2_v, 1, (zero_edge, zero_edge))
    second_halo = halo_copies(1)
    for copy in second_halo:
        copy.start()
    for copy in second_halo:
        copy.wait_recv()
    edge_columns(1)
    edge_rows(1)

    def put_second(layer, c, r0, value):
        out_v[pl.ds(pl.multiple_of((layer * NC + c) * CY + r0, ROWS), ROWS), :] = value

    def out_copy(layer):
        rows = pl.ds(pl.multiple_of(layer * NC * CY, NC * CY), NC * CY)
        return pltpu.make_async_copy(out_v.at[rows], out_h.at[rows], out_sem.at[layer])

    def second_layer(layer, carry):
        blocks(layer, 1, s2_v, put_second)
        out_copy(layer).start()
        return carry

    lax.fori_loop(0, LAYERS, second_layer, 0)

    some = gb.at[pl.ds(0, WY - 1)]
    grad_copy(some, some, (gx, lax.rem(gy + 1, WY)), 1).wait_recv()
    total = gb[0]
    for i in range(1, WY):
        total = total + gb[i]
    scale = -1.0 / math.sqrt(BLK * BLOCKS * DEVICES)
    grad_ref[...] = scale * total[:, :NC]

    for copy in first_halo + second_halo:
        copy.wait_send()
    some = ga.at[pl.ds(0, WX - 1)]
    grad_copy(some, some, (lax.rem(gx + 1, WX), gy), 0).wait_send()
    some = gb.at[pl.ds(0, WY - 1)]
    grad_copy(some, some, (gx, lax.rem(gy + 1, WY)), 1).wait_send()

    def drain(chunk, carry):
        wait_chunk(ps, rb, chunk, ps_send, ps_recv, True)
        wait_chunk(cs, cr, chunk, cs_send, cs_recv, True)
        return carry

    lax.fori_loop(0, CHUNKS, drain, 0)

    def drain_out(layer, carry):
        out_copy(layer).wait()
        return carry

    lax.fori_loop(0, LAYERS, drain_out, 0)


def shards(
    cotangent, permeability, well_mask, diag_block, flux_block, cell_list, block_count, helper_of,
    flash_inverse, flash_coupling, phase_state,
):
    any_space = pl.BlockSpec(memory_space=pl.ANY)
    vmem = pl.BlockSpec(memory_space=pltpu.VMEM)
    smem = pl.BlockSpec(memory_space=pltpu.SMEM)
    dma = pltpu.SemaphoreType.DMA
    adjoint, grad = pl.pallas_call(
        kernel,
        out_shape=(
            jax.ShapeDtypeStruct((FIELDS * CY, CX), F32),
            jax.ShapeDtypeStruct((NC, NC), F32),
        ),
        in_specs=[any_space] * 5 + [vmem, smem, vmem] + [any_space] * 3,
        out_specs=(any_space, vmem),
        scratch_shapes=[
            pltpu.VMEM((FIELDS * CY, CX), F32),
            pltpu.VMEM((LAYERS * CY, CX), F32),
            pltpu.VMEM((CY, CX), jnp.int32),
            pltpu.VMEM((LAYERS, NC, NC, CY, CX), BF16),
            pltpu.VMEM((LAYERS, NC, NC, CY, CX), BF16),
            pltpu.VMEM((BLOCKS, NC, NC, BLK), BF16),
            pltpu.VMEM((BLOCKS, NC, NC, BLK), BF16),
            pltpu.VMEM((BLOCKS, NC, BLK), BF16),
            pltpu.VMEM(((FIELDS + 2 * NC) * PAD, CX), F32),
            pltpu.VMEM(((LAYERS + 2) * PAD, CX), F32),
            pltpu.VMEM((6, LAYERS * CY, CX), F32),
            pltpu.VMEM((NC * CY, LAYERS * CX), BF16),
            pltpu.VMEM((FIELDS * CY, CX), F32),
            pltpu.VMEM((BLOCKS, BLK), F32),
            pltpu.VMEM((BLOCKS, BLK), F32),
            pltpu.VMEM((LAYERS * CX, NB * BLK), BF16),
            pltpu.VMEM((NC * CY, NB * BLK), BF16),
            pltpu.VMEM((BLOCKS, NC, BLK), BF16),
            pltpu.VMEM((BLOCKS, NC, BLK), BF16),
            pltpu.VMEM((BLOCKS, NC, BLK), BF16),
            pltpu.VMEM((BLOCKS, NC, BLK), BF16),
            pltpu.VMEM((NC, NC, BLK), F32),
            pltpu.VMEM((NC, CX), F32),
            pltpu.VMEM((WX, NC, CX), F32),
            pltpu.VMEM((NC, CX), F32),
            pltpu.VMEM((WY, NC, CX), F32),
            pltpu.VMEM((2, 2, CY, CX), F32),
            pltpu.VMEM((2, 2, CY, CX), F32),
            pltpu.VMEM((2, 2, 56, CX), F32),
            pltpu.VMEM((2, 2, 56, CX), F32),
            pltpu.VMEM((FIELDS * CY, CX), F32),
            dma((3,)),
            dma((2, LAYERS)),
            dma((3,)),
            dma((LAYERS,)),
            dma((2, 4)),
            dma((2, 4)),
            dma((CHUNKS,)),
            dma((CHUNKS,)),
            dma((CHUNKS,)),
            dma((CHUNKS,)),
            dma((2,)),
            dma((2,)),
        ],
        compiler_params=pltpu.CompilerParams(
            collective_id=0, has_side_effects=True, vmem_limit_bytes=60 << 20
        ),
    )(
        cotangent.reshape(FIELDS * CY, CX),
        permeability.reshape(LAYERS * CY, CX),
        well_mask,
        diag_block,
        flux_block,
        cell_list.reshape(BLOCKS, BLK),
        block_count,
        helper_of.reshape(1, BLOCKS),
        flash_inverse.reshape(BLOCKS, NC, NC, BLK),
        flash_coupling.reshape(BLOCKS, NC, NC, BLK),
        phase_state.reshape(BLOCKS, NC, BLK),
    )
    return adjoint.reshape(cotangent.shape), grad


def solution(mesh):
    return jax.shard_map(
        shards,
        mesh=mesh,
        in_specs=(
            P(None, None, "gy", "gx"),
            P(None, "gy", "gx"),
            P("gy", "gx"),
            P(None, None, None, "gy", "gx"),
            P(None, None, None, "gy", "gx"),
            P("gy", "gx", None),
            P("gy", "gx"),
            P("gy", "gx", None),
            P("gy", "gx", None, None, None, None),
            P("gy", "gx", None, None, None, None),
            P("gy", "gx", None, None, None),
        ),
        out_specs=(P(None, None, "gy", "gx"), P()),
        check_vma=False,
    )
```

```python
import functools
import math

import jax
import jax.numpy as jnp
from jax import lax
from jax.experimental import pallas as pl
from jax.experimental.pallas import tpu as pltpu
from jax.sharding import PartitionSpec as P

MESH = pl.DeviceIdType.MESH
F32 = jnp.float32
BF16 = jnp.bfloat16

LAYERS, NC, CY, CX = 6, 8, 64, 128
FIELDS = LAYERS * NC
PAD = 80
WX, WY = 8, 16
DEVICES = WX * WY
BLOCKS, BLK = 128, 128
NB = 8
CHUNKS = BLOCKS // NB
DELAY = 5
ROWS = 16


def kernel(
    cot_h, perm_h, mask_h, diag_h, flux_h, cells_h, count_ref, helper_h, inv_h, coup_h, phase_h,
    out_v, grad_ref,
    cot_v, perm_v, mask_v, cells_ref, helper_ref, diag_v, flux_v, inv_v, coup_v, phase_v,
    w_v, k_v, t_v, f16_v, s2_v, code_v, y_v, oh_v, lhs_v,
    ps, rb, cs, cr, g_v, gt, ga, gt2, gb,
    hx_s, hx_r, hy_s, hy_r,
    load_sem, blk_sem, fl_sem,
    halo_send, halo_recv, ps_send, ps_recv, cs_send, cs_recv, g_send, g_recv,
):
    gx = lax.axis_index("gx")
    gy = lax.axis_index("gy")
    me = gx * WY + gy

    def device(linear):
        return (lax.div(linear, WY), lax.rem(linear, WY))

    loads = [
        pltpu.make_async_copy(cot_h, cot_v, load_sem.at[0]),
        pltpu.make_async_copy(perm_h, perm_v, load_sem.at[1]),
        pltpu.make_async_copy(mask_h, mask_v, load_sem.at[2]),
    ]
    table_loads = [
        pltpu.make_async_copy(cells_h, cells_ref, load_sem.at[3]),
        pltpu.make_async_copy(helper_h, helper_ref, load_sem.at[4]),
    ]
    for copy in loads + table_loads:
        copy.start()

    def block_copy(which, layer):
        source, held = ((diag_h, diag_v), (flux_h, flux_v))[which]
        return pltpu.make_async_copy(source.at[layer], held.at[layer], blk_sem.at[which, layer])

    for which in range(2):
        for layer in range(LAYERS):
            block_copy(which, layer).start()
    flash_loads = [
        pltpu.make_async_copy(inv_h, inv_v, fl_sem.at[0]),
        pltpu.make_async_copy(coup_h, coup_v, fl_sem.at[1]),
        pltpu.make_async_copy(phase_h, phase_v, fl_sem.at[2]),
    ]
    for copy in flash_loads:
        copy.start()

    barrier = pltpu.get_barrier_semaphore()

    def greet(step, carry):
        pl.semaphore_signal(
            barrier, inc=1, device_id=device(lax.rem(me + step, DEVICES)), device_id_type=MESH
        )
        return carry

    lax.fori_loop(1, DEVICES, greet, 0)

    for copy in table_loads:
        copy.wait()
    lane_i = lax.broadcasted_iota(jnp.int32, (BLOCKS, BLK), 1)
    row_i = lax.broadcasted_iota(jnp.int32, (BLOCKS, BLK), 0)
    target = lax.rem(row_i + me + 1, DEVICES)
    choose = jnp.where(helper_ref[...] == target, 1.0, 0.0).astype(BF16)
    cells = cells_ref[...]
    cell_layer = lax.shift_right_logical(cells, 13).astype(F32).astype(BF16)
    cell_y = lax.shift_right_logical(cells, 7) & (CY - 1)
    cell_y = jnp.where(row_i < count_ref[0, 0], cell_y, CY).astype(F32).astype(BF16)
    cell_x = (cells & (CX - 1)).astype(F32).astype(BF16)
    code_v[...] = CX * jnp.dot(choose, cell_layer, preferred_element_type=F32) + jnp.dot(
        choose, cell_x, preferred_element_type=F32
    )
    y_v[...] = jnp.dot(choose, cell_y, preferred_element_type=F32)

    w_v[pl.ds(0, NC * PAD), :] = jnp.zeros((NC * PAD, CX), F32)
    w_v[pl.ds((FIELDS + NC) * PAD, NC * PAD), :] = jnp.zeros((NC * PAD, CX), F32)
    k_v[pl.ds(0, PAD), :] = jnp.zeros((PAD, CX), F32)
    k_v[pl.ds((LAYERS + 1) * PAD, PAD), :] = jnp.zeros((PAD, CX), F32)

    for copy in loads:
        copy.wait()

    lane_y = lax.broadcasted_iota(jnp.int32, (CY, CX), 1)
    hole = mask_v[...].astype(F32)
    keep = 1.0 - hole

    def field(q):
        return pl.ds(pl.multiple_of(q * CY, CY), CY)

    def pack_edges(q, value, carry):
        right, left = carry
        turned = pltpu.roll(value, 2 * q + 2, axis=1)
        right = jnp.where(lane_y == 2 * q + 1, turned, right)
        left = jnp.where(lane_y == 2 * q + 2, turned, left)
        return right, left

    def mask_fields(source, which, start):
        def step(q, carry):
            value = source[field(q), :] * keep
            w_v[pl.ds(pl.multiple_of((q + NC) * PAD + 8, 8), CY), :] = value
            return pack_edges(q, value, carry)

        right, left = lax.fori_loop(0, FIELDS, step, start, unroll=2)
        hx_s[which, 0] = left
        hx_s[which, 1] = right
        for layer in range(LAYERS):
            base = (layer + 1) * NC * PAD + 8
            hy_s[which, 0, pl.ds(layer * NC, NC), :] = w_v[pl.ds(base, NC, stride=PAD), :]
            hy_s[which, 1, pl.ds(layer * NC, NC), :] = w_v[pl.ds(base + CY - 1, NC, stride=PAD), :]

    def halo_copies(which):
        east = (lax.rem(gx + 1, WX), gy)
        west = (lax.rem(gx + WX - 1, WX), gy)
        south = (gx, lax.rem(gy + 1, WY))
        north = (gx, lax.rem(gy + WY - 1, WY))
        plan = (
            (hx_s.at[which, 1], hx_r.at[which, 0], east),
            (hx_s.at[which, 0], hx_r.at[which, 1], west),
            (hy_s.at[which, 1], hy_r.at[which, 0], south),
            (hy_s.at[which, 0], hy_r.at[which, 1], north),
        )
        return [
            pltpu.make_async_remote_copy(
                src_ref=source,
                dst_ref=target_ref,
                send_sem=halo_send.at[which, i],
                recv_sem=halo_recv.at[which, i],
                device_id=where,
                device_id_type=MESH,
            )
            for i, (source, target_ref, where) in enumerate(plan)
        ]

    def edge_columns(which):
        odd = lax.rem(lane_y, 2) == 1
        from_west = jnp.where(gx > 0, hx_r[which, 0], 0.0)
        from_east = jnp.where(gx < WX - 1, hx_r[which, 1], 0.0)
        hx_r[which, 0] = jnp.where(odd, from_west, from_east)

    def edge_rows(which):
        for layer in range(LAYERS):
            base = (layer + 1) * NC * PAD
            rows = pl.ds(layer * NC, NC)
            w_v[pl.ds(base + 7, NC, stride=PAD), :] = jnp.where(gy > 0, hy_r[which, 0, rows, :], 0.0)
            w_v[pl.ds(base + 8 + CY, NC, stride=PAD), :] = jnp.where(
                gy < WY - 1, hy_r[which, 1, rows, :], 0.0
            )

    zero_edge = jnp.zeros((CY, CX), F32)
    start = (zero_edge, zero_edge)
    for layer in range(LAYERS):
        value = perm_v[pl.ds(layer * CY, CY), :]
        k_v[pl.ds((layer + 1) * PAD + 8, CY), :] = value
        start = pack_edges(FIELDS + layer, value, start)
    mask_fields(cot_v, 0, start)
    for layer in range(LAYERS):
        base = (layer + 1) * PAD + 8
        hy_s[0, 0, pl.ds(FIELDS + layer, 1), :] = k_v[pl.ds(base, 1), :]
        hy_s[0, 1, pl.ds(FIELDS + layer, 1), :] = k_v[pl.ds(base + CY - 1, 1), :]

    pl.semaphore_wait(barrier, DEVICES - 1)
    first_halo = halo_copies(0)
    for copy in first_halo:
        copy.start()

    def beside_x(value, edges, shift, lane):
        turned = pltpu.roll(edges, shift, axis=1)
        west = pltpu.roll(jnp.where(lane == CX - 1, turned, value), 1, axis=1)
        east = pltpu.roll(jnp.where(lane == 0, turned, value), CX - 1, axis=1)
        return west, east

    def make_weights(layer, carry):
        base = pl.multiple_of((layer + 1) * PAD, 8)
        centre = k_v[pl.ds(base + 8, CY), :]
        west, east = beside_x(centre, hx_r[0, 0], CX - 2 * (FIELDS + layer) - 2, lane_y)
        others = (
            k_v[pl.ds(base + 8 + PAD, CY), :],
            k_v[pl.ds(base + 8 - PAD, CY), :],
            k_v[pl.ds(base + 9, CY), :],
            k_v[pl.ds(base + 7, CY), :],
            east,
            west,
        )
        for i, other in enumerate(others):
            t_v[i, field(layer), :] = 2.0 * centre * other / (centre + other)
        return carry

    lane_r = lax.broadcasted_iota(jnp.int32, (ROWS, CX), 1)

    def part_rows(layer, c, r0):
        return pl.ds(pl.multiple_of((layer * NC + c) * CY + r0, ROWS), ROWS)

    def diag_pass(layer, source, held):
        for r0 in range(0, CY, ROWS):
            well = mask_v[pl.ds(r0, ROWS), :].astype(F32)
            acc = [well * source[part_rows(layer, c, r0), :] for c in range(NC)]
            for r in range(NC):
                base = pl.multiple_of((layer + 1) * (NC * PAD) + (r * PAD + 8 + r0), 8)
                own = w_v[pl.ds(base, ROWS), :]
                for c in range(NC):
                    acc[c] = acc[c] + diag_v[layer, r, c, pl.ds(r0, ROWS), :].astype(F32) * own
            for c in range(NC):
                held[part_rows(layer, c, r0), :] = acc[c]

    def flux_pass(layer, which, held, put):
        for r0 in range(0, CY, ROWS):
            rows = pl.ds(pl.multiple_of(layer * CY + r0, ROWS), ROWS)
            weights = [t_v[i, rows, :] for i in range(6)]
            edges = hx_r[which, 0, pl.ds(r0, ROWS), :]
            acc = [held[part_rows(layer, c, r0), :] for c in range(NC)]
            for r in range(NC):
                base = pl.multiple_of((layer + 1) * (NC * PAD) + (r * PAD + 8 + r0), 8)
                value = w_v[pl.ds(base, ROWS), :]
                west, east = beside_x(value, edges, CX - 2 * (layer * NC + r) - 2, lane_r)
                total = weights[0] * w_v[pl.ds(base + NC * PAD, ROWS), :]
                total = total + weights[1] * w_v[pl.ds(base - NC * PAD, ROWS), :]
                total = total + weights[2] * w_v[pl.ds(base + 1, ROWS), :]
                total = total + weights[3] * w_v[pl.ds(base - 1, ROWS), :]
                total = total + weights[4] * east
                total = total + weights[5] * west
                for c in range(NC):
                    acc[c] = acc[c] - flux_v[layer, r, c, pl.ds(r0, ROWS), :].astype(F32) * total
            for c in range(NC):
                put(layer, c, r0, acc[c])

    def put_first(layer, c, r0, value):
        lanes = pl.ds(pl.multiple_of(layer * CX, CX), CX)
        f16_v[pl.ds(c * CY + r0, ROWS), lanes] = value.astype(BF16)
        s2_v[part_rows(layer, c, r0), :] = value

    def first_diag(layer, carry):
        block_copy(0, layer).wait()
        diag_pass(layer, cot_v, s2_v)
        return carry

    def first_flux(layer, carry):
        block_copy(1, layer).wait()
        flux_pass(layer, 0, s2_v, put_first)
        return carry

    lax.fori_loop(0, LAYERS, first_diag, 0)

    for copy in first_halo:
        copy.wait_recv()
    edge_columns(0)
    edge_rows(0)
    for layer in range(LAYERS):
        base = (layer + 1) * PAD
        k_v[pl.ds(base + 7, 1), :] = jnp.where(gy > 0, hy_r[0, 0, pl.ds(FIELDS + layer, 1), :], 0.0)
        k_v[pl.ds(base + 8 + CY, 1), :] = jnp.where(
            gy < WY - 1, hy_r[0, 1, pl.ds(FIELDS + layer, 1), :], 0.0
        )
    lax.fori_loop(0, LAYERS, make_weights, 0)
    lax.fori_loop(0, LAYERS, first_flux, 0)
    for copy in flash_loads:
        copy.wait()

    iota_x = lax.broadcasted_iota(jnp.int32, (CX, BLK), 0).astype(F32).astype(BF16)
    iota_y = lax.broadcasted_iota(jnp.int32, (CY, BLK), 0).astype(F32)
    one16 = jnp.ones((CX, BLK), BF16)
    zero16 = jnp.zeros((CX, BLK), BF16)

    def one_hot(p, b):
        code = code_v[pl.ds(p, 1), :]
        for layer in range(LAYERS):
            own_x = jnp.broadcast_to((code - float(layer * CX)).astype(BF16), (CX, BLK))
            oh_v[pl.ds(layer * CX, CX), pl.ds(b * BLK, BLK)] = jnp.where(own_x == iota_x, one16, zero16)

    def send_chunk(buf, to, chunk, sign, send, recv):
        for b in range(NB):
            p = chunk * NB + b

            def remote():
                pltpu.make_async_remote_copy(
                    src_ref=buf.at[p],
                    dst_ref=to.at[p],
                    send_sem=send.at[chunk],
                    recv_sem=recv.at[chunk],
                    device_id=device(lax.rem(me + sign * (p + 1) + DEVICES, DEVICES)),
                    device_id_type=MESH,
                ).start()

            if b < NB - 1:
                remote()
            else:
                pl.when(chunk < CHUNKS - 1)(remote)

                @pl.when(chunk == CHUNKS - 1)
                def _():
                    pltpu.make_async_copy(buf.at[p], to.at[p], recv.at[chunk]).start()

    def chunk_copy(buf, to, chunk, count, send, recv):
        rows = pl.ds(chunk * NB, count)
        return pltpu.make_async_remote_copy(
            src_ref=buf.at[rows],
            dst_ref=to.at[rows],
            send_sem=send.at[chunk],
            recv_sem=recv.at[chunk],
            device_id=device(lax.rem(me + 1, DEVICES)),
            device_id_type=MESH,
        )

    def gather(chunk):
        for b in range(NB):
            one_hot(chunk * NB + b, b)
        wide = jnp.dot(f16_v[...], oh_v[...], preferred_element_type=F32)
        for b in range(NB):
            p = chunk * NB + b
            hit = jnp.broadcast_to(y_v[pl.ds(p, 1), :], (CY, BLK)) == iota_y
            found = []
            for c in range(NC):
                piece = wide[c * CY : (c + 1) * CY, b * BLK : (b + 1) * BLK]
                found.append(jnp.sum(jnp.where(hit, piece, 0.0), axis=0, keepdims=True))
            ps[p] = jnp.concatenate(found, axis=0).astype(BF16)

    def flash(chunk):
        total = g_v[...]
        for b in range(NB):
            p = chunk * NB + b
            source = lax.rem(me - (p + 1) + DEVICES, DEVICES)
            chosen = rb[p].astype(F32)
            multiplier = jnp.sum(inv_v[source].astype(F32) * chosen[:, None, :], axis=0)
            change = -jnp.sum(coup_v[source].astype(F32) * multiplier[:, None, :], axis=0)
            state = phase_v[source].astype(F32)
            total = total + (multiplier * state)[None] * state[:, None, :]
            cs[p] = change.astype(BF16)
        g_v[...] = total

    def scatter(chunk):
        for b in range(NB):
            p = chunk * NB + b
            one_hot(p, b)
            hit = jnp.broadcast_to(y_v[pl.ds(p, 1), :], (CY, BLK)) == iota_y
            change = cr[p].astype(F32)
            for c in range(NC):
                lhs_v[pl.ds(c * CY, CY), pl.ds(b * BLK, BLK)] = jnp.where(
                    hit, jnp.broadcast_to(change[c : c + 1], (CY, BLK)), 0.0
                ).astype(BF16)
        added = lax.dot_general(
            lhs_v[...], oh_v[...], (((1,), (1,)), ((), ())), preferred_element_type=F32
        )
        for layer in range(LAYERS):
            rows = pl.ds(layer * NC * CY, NC * CY)
            s2_v[rows, :] = s2_v[rows, :] + added[:, layer * CX : (layer + 1) * CX]

    g_v[...] = jnp.zeros_like(g_v)

    def loop(low, high, gathers=None, flashes=None, scatters=None):
        def body(t, carry):
            if flashes is not None:
                chunk_copy(ps, rb, t - flashes, NB, ps_send, ps_recv).wait_recv()
            if scatters is not None:
                chunk_copy(cs, cr, t - scatters, NB, cs_send, cs_recv).wait_recv()
            if gathers is not None:
                gather(t - gathers)
            if flashes is not None:
                flash(t - flashes)
            if scatters is not None:
                scatter(t - scatters)
            if gathers is not None:
                send_chunk(ps, rb, t - gathers, 1, ps_send, ps_recv)
            if flashes is not None:
                send_chunk(cs, cr, t - flashes, -1, cs_send, cs_recv)
            return carry

        lax.fori_loop(low, high, body, 0)

    loop(0, DELAY, gathers=0)
    loop(DELAY, CHUNKS, gathers=0, flashes=DELAY)
    loop(CHUNKS, CHUNKS + DELAY, flashes=DELAY, scatters=CHUNKS)

    lane_g = lax.broadcasted_iota(jnp.int32, (NC, CX), 1)
    tile = jnp.zeros((NC, CX), F32)
    for j in range(NC):
        tile = jnp.where(lane_g == j, jnp.sum(g_v[j], axis=1, keepdims=True), tile)
    gt[...] = tile
    ga[gx] = tile

    def grad_copy(source, target_ref, where, phase):
        return pltpu.make_async_remote_copy(
            src_ref=source,
            dst_ref=target_ref,
            send_sem=g_send.at[phase],
            recv_sem=g_recv.at[phase],
            device_id=where,
            device_id_type=MESH,
        )

    def send_x(step, carry):
        grad_copy(gt, ga.at[gx], (lax.rem(gx + step, WX), gy), 0).start()
        return carry

    lax.fori_loop(1, WX, send_x, 0)

    loop(CHUNKS + DELAY, 2 * CHUNKS, scatters=CHUNKS)

    some = ga.at[pl.ds(0, WX - 1)]
    grad_copy(some, some, (lax.rem(gx + 1, WX), gy), 0).wait_recv()
    part = ga[0]
    for i in range(1, WX):
        part = part + ga[i]
    gt2[...] = part
    gb[gy] = part

    def send_y(step, carry):
        grad_copy(gt2, gb.at[gy], (gx, lax.rem(gy + step, WY)), 1).start()
        return carry

    lax.fori_loop(1, WY, send_y, 0)

    mask_fields(s2_v, 1, (zero_edge, zero_edge))
    second_halo = halo_copies(1)
    for copy in second_halo:
        copy.start()

    def second_diag(layer, carry):
        diag_pass(layer, s2_v, out_v)
        return carry

    lax.fori_loop(0, LAYERS, second_diag, 0)
    for copy in second_halo:
        copy.wait_recv()
    edge_columns(1)
    edge_rows(1)

    def put_second(layer, c, r0, value):
        out_v[part_rows(layer, c, r0), :] = value

    def second_flux(layer, carry):
        flux_pass(layer, 1, out_v, put_second)
        return carry

    lax.fori_loop(0, LAYERS, second_flux, 0)

    some = gb.at[pl.ds(0, WY - 1)]
    grad_copy(some, some, (gx, lax.rem(gy + 1, WY)), 1).wait_recv()
    total = gb[0]
    for i in range(1, WY):
        total = total + gb[i]
    scale = -1.0 / math.sqrt(BLK * BLOCKS * DEVICES)
    grad_ref[...] = scale * total[:, :NC]

    for copy in first_halo + second_halo:
        copy.wait_send()
    some = ga.at[pl.ds(0, WX - 1)]
    grad_copy(some, some, (lax.rem(gx + 1, WX), gy), 0).wait_send()
    some = gb.at[pl.ds(0, WY - 1)]
    grad_copy(some, some, (gx, lax.rem(gy + 1, WY)), 1).wait_send()

    def drain(chunk, carry):
        chunk_copy(ps, rb, chunk, NB, ps_send, ps_recv).wait_send()
        chunk_copy(cs, cr, chunk, NB, cs_send, cs_recv).wait_send()
        return carry

    lax.fori_loop(0, CHUNKS - 1, drain, 0)
    chunk_copy(ps, rb, CHUNKS - 1, NB - 1, ps_send, ps_recv).wait_send()
    chunk_copy(cs, cr, CHUNKS - 1, NB - 1, cs_send, cs_recv).wait_send()


def shards(
    cotangent, permeability, well_mask, diag_block, flux_block, cell_list, block_count, helper_of,
    flash_inverse, flash_coupling, phase_state,
):
    hbm = pl.BlockSpec(memory_space=pltpu.HBM)
    smem = pl.BlockSpec(memory_space=pltpu.SMEM)
    vmem = pl.BlockSpec(memory_space=pltpu.VMEM)
    dma = pltpu.SemaphoreType.DMA
    def pin(array):
        return pltpu.with_memory_space_constraint(array, pltpu.HBM)

    adjoint, grad = pl.pallas_call(
        kernel,
        out_shape=(
            pltpu.VMEM((FIELDS * CY, CX), F32),
            pltpu.VMEM((NC, NC), F32),
        ),
        in_specs=[hbm] * 6 + [smem] + [hbm] * 4,
        out_specs=(vmem, vmem),
        scratch_shapes=[
            pltpu.VMEM((FIELDS * CY, CX), F32),
            pltpu.VMEM((LAYERS * CY, CX), F32),
            pltpu.VMEM((CY, CX), jnp.int32),
            pltpu.VMEM((BLOCKS, BLK), jnp.int32),
            pltpu.VMEM((1, BLOCKS), jnp.int32),
            pltpu.VMEM((LAYERS, NC, NC, CY, CX), BF16),
            pltpu.VMEM((LAYERS, NC, NC, CY, CX), BF16),
            pltpu.VMEM((BLOCKS, NC, NC, BLK), BF16),
            pltpu.VMEM((BLOCKS, NC, NC, BLK), BF16),
            pltpu.VMEM((BLOCKS, NC, BLK), BF16),
            pltpu.VMEM(((FIELDS + 2 * NC) * PAD, CX), F32),
            pltpu.VMEM(((LAYERS + 2) * PAD, CX), F32),
            pltpu.VMEM((6, LAYERS * CY, CX), F32),
            pltpu.VMEM((NC * CY, LAYERS * CX), BF16),
            pltpu.VMEM((FIELDS * CY, CX), F32),
            pltpu.VMEM((BLOCKS, BLK), F32),
            pltpu.VMEM((BLOCKS, BLK), F32),
            pltpu.VMEM((LAYERS * CX, NB * BLK), BF16),
            pltpu.VMEM((NC * CY, NB * BLK), BF16),
            pltpu.VMEM((BLOCKS, NC, BLK), BF16),
            pltpu.VMEM((BLOCKS, NC, BLK), BF16),
            pltpu.VMEM((BLOCKS, NC, BLK), BF16),
            pltpu.VMEM((BLOCKS, NC, BLK), BF16),
            pltpu.VMEM((NC, NC, BLK), F32),
            pltpu.VMEM((NC, CX), F32),
            pltpu.VMEM((WX, NC, CX), F32),
            pltpu.VMEM((NC, CX), F32),
            pltpu.VMEM((WY, NC, CX), F32),
            pltpu.VMEM((2, 2, CY, CX), F32),
            pltpu.VMEM((2, 2, CY, CX), F32),
            pltpu.VMEM((2, 2, 56, CX), F32),
            pltpu.VMEM((2, 2, 56, CX), F32),
            dma((5,)),
            dma((2, LAYERS)),
            dma((3,)),
            dma((2, 4)),
            dma((2, 4)),
            dma((CHUNKS,)),
            dma((CHUNKS,)),
            dma((CHUNKS,)),
            dma((CHUNKS,)),
            dma((2,)),
            dma((2,)),
        ],
        compiler_params=pltpu.CompilerParams(
            collective_id=0, has_side_effects=True, vmem_limit_bytes=50 << 20
        ),
    )(
        pin(cotangent.reshape(FIELDS * CY, CX)),
        pin(permeability.reshape(LAYERS * CY, CX)),
        pin(well_mask),
        pin(diag_block),
        pin(flux_block),
        pin(cell_list.reshape(BLOCKS, BLK)),
        block_count,
        pin(helper_of.reshape(1, BLOCKS)),
        pin(flash_inverse.reshape(BLOCKS, NC, NC, BLK)),
        pin(flash_coupling.reshape(BLOCKS, NC, NC, BLK)),
        pin(phase_state.reshape(BLOCKS, NC, BLK)),
    )
    return adjoint.reshape(cotangent.shape), grad


def solution(mesh):
    return jax.shard_map(
        shards,
        mesh=mesh,
        in_specs=(
            P(None, None, "gy", "gx"),
            P(None, "gy", "gx"),
            P("gy", "gx"),
            P(None, None, None, "gy", "gx"),
            P(None, None, None, "gy", "gx"),
            P("gy", "gx", None),
            P("gy", "gx"),
            P("gy", "gx", None),
            P("gy", "gx", None, None, None, None),
            P("gy", "gx", None, None, None, None),
            P("gy", "gx", None, None, None),
        ),
        out_specs=(P(None, None, "gy", "gx"), P()),
        check_vma=False,
    )
```

```python
import functools
import math

import jax
import jax.numpy as jnp
from jax import lax
from jax.experimental import pallas as pl
from jax.experimental.pallas import tpu as pltpu
from jax.sharding import PartitionSpec as P

MESH = pl.DeviceIdType.MESH
F32 = jnp.float32
BF16 = jnp.bfloat16

LAYERS, NC, CY, CX = 6, 8, 64, 128
FIELDS = LAYERS * NC
PAD = 80
WX, WY = 8, 16
DEVICES = WX * WY
BLOCKS, BLK = 128, 128
NB = 16
SUB = 8
CHUNKS = BLOCKS // NB
DELAY = 4
ROWS = 16


def kernel(
    cot_h, perm_h, mask_h, diag_h, flux_h, cells_h, count_ref, helper_h, inv_h, coup_h, phase_h,
    out_v, grad_ref,
    cot_v, perm_v, mask_v, cells_ref, helper_ref, diag_v, flux_v, inv_v, coup_v, phase_v,
    w_v, west_v, east_v, k_v, t_v, f16_v, s2_v, code_v, y_v, oh_v, lhs_v,
    ps, rb, cs, cr, g_v, gt, ga, gt2, gb,
    hx_s, hx_r, hy_s, hy_r,
    load_sem, blk_sem, fl_sem,
    halo_send, halo_recv, ps_send, ps_recv, cs_send, cs_recv, g_send, g_recv,
):
    gx = lax.axis_index("gx")
    gy = lax.axis_index("gy")
    me = gx * WY + gy

    def device(linear):
        return (lax.div(linear, WY), lax.rem(linear, WY))

    barrier = pltpu.get_barrier_semaphore()

    def greet(step, carry):
        pl.semaphore_signal(
            barrier, inc=1, device_id=device(lax.rem(me + step, DEVICES)), device_id_type=MESH
        )
        return carry

    lax.fori_loop(1, DEVICES, greet, 0)

    loads = [
        pltpu.make_async_copy(cot_h, cot_v, load_sem.at[0]),
        pltpu.make_async_copy(perm_h, perm_v, load_sem.at[1]),
        pltpu.make_async_copy(mask_h, mask_v, load_sem.at[2]),
    ]
    table_loads = [
        pltpu.make_async_copy(cells_h, cells_ref, load_sem.at[3]),
        pltpu.make_async_copy(helper_h, helper_ref, load_sem.at[4]),
    ]
    for copy in loads + table_loads:
        copy.start()

    def block_copy(which, layer):
        source, held = ((diag_h, diag_v), (flux_h, flux_v))[which]
        return pltpu.make_async_copy(source.at[layer], held.at[layer], blk_sem.at[which, layer])

    for which in range(2):
        for layer in range(LAYERS):
            block_copy(which, layer).start()
    flash_loads = [
        pltpu.make_async_copy(inv_h, inv_v, fl_sem.at[0]),
        pltpu.make_async_copy(coup_h, coup_v, fl_sem.at[1]),
        pltpu.make_async_copy(phase_h, phase_v, fl_sem.at[2]),
    ]
    for copy in flash_loads:
        copy.start()

    w_v[pl.ds(0, NC * PAD), :] = jnp.zeros((NC * PAD, CX), F32)
    w_v[pl.ds((FIELDS + NC) * PAD, NC * PAD), :] = jnp.zeros((NC * PAD, CX), F32)
    k_v[pl.ds(0, PAD), :] = jnp.zeros((PAD, CX), F32)
    k_v[pl.ds((LAYERS + 1) * PAD, PAD), :] = jnp.zeros((PAD, CX), F32)

    for copy in loads:
        copy.wait()

    lane_y = lax.broadcasted_iota(jnp.int32, (CY, CX), 1)
    hole = mask_v[...].astype(F32)
    keep = 1.0 - hole

    def field(q):
        return pl.ds(pl.multiple_of(q * CY, CY), CY)

    def pack_edges(q, value, carry):
        right, left = carry
        turned = pltpu.roll(value, 2 * q + 2, axis=1)
        right = jnp.where(lane_y == 2 * q + 1, turned, right)
        left = jnp.where(lane_y == 2 * q + 2, turned, left)
        return right, left

    def mask_fields(source, which, start):
        def step(q, carry):
            value = source[field(q), :] * keep
            w_v[pl.ds(pl.multiple_of((q + NC) * PAD + 8, 8), CY), :] = value
            return pack_edges(q, value, carry)

        right, left = lax.fori_loop(0, FIELDS, step, start, unroll=8)
        hx_s[which, 0] = pltpu.roll(left, CX - 2, axis=1)
        hx_s[which, 1] = right
        for layer in range(LAYERS):
            base = (layer + 1) * NC * PAD + 8
            hy_s[which, 0, pl.ds(layer * NC, NC), :] = w_v[pl.ds(base, NC, stride=PAD), :]
            hy_s[which, 1, pl.ds(layer * NC, NC), :] = w_v[pl.ds(base + CY - 1, NC, stride=PAD), :]

    def halo_copies(which):
        east = (lax.rem(gx + 1, WX), gy)
        west = (lax.rem(gx + WX - 1, WX), gy)
        south = (gx, lax.rem(gy + 1, WY))
        north = (gx, lax.rem(gy + WY - 1, WY))
        plan = (
            (hx_s.at[which, 1], hx_r.at[which, 0], east),
            (hx_s.at[which, 0], hx_r.at[which, 1], west),
            (hy_s.at[which, 1], hy_r.at[which, 0], south),
            (hy_s.at[which, 0], hy_r.at[which, 1], north),
        )
        return [
            pltpu.make_async_remote_copy(
                src_ref=source,
                dst_ref=target_ref,
                send_sem=halo_send.at[which, i],
                recv_sem=halo_recv.at[which, i],
                device_id=where,
                device_id_type=MESH,
            )
            for i, (source, target_ref, where) in enumerate(plan)
        ]

    def edge_columns(which):
        odd = lax.rem(lane_y, 2) == 1
        from_west = jnp.where(gx > 0, hx_r[which, 0], 0.0)
        from_east = jnp.where(gx < WX - 1, hx_r[which, 1], 0.0)
        hx_r[which, 0] = jnp.where(odd, from_west, from_east)

    def edge_rows(which):
        for layer in range(LAYERS):
            base = (layer + 1) * NC * PAD
            rows = pl.ds(layer * NC, NC)
            w_v[pl.ds(base + 7, NC, stride=PAD), :] = jnp.where(gy > 0, hy_r[which, 0, rows, :], 0.0)
            w_v[pl.ds(base + 8 + CY, NC, stride=PAD), :] = jnp.where(
                gy < WY - 1, hy_r[which, 1, rows, :], 0.0
            )

    zero_edge = jnp.zeros((CY, CX), F32)
    start = (zero_edge, zero_edge)
    for layer in range(LAYERS):
        value = perm_v[pl.ds(layer * CY, CY), :]
        k_v[pl.ds((layer + 1) * PAD + 8, CY), :] = value
        start = pack_edges(FIELDS + layer, value, start)
    mask_fields(cot_v, 0, start)
    for layer in range(LAYERS):
        base = (layer + 1) * PAD + 8
        hy_s[0, 0, pl.ds(FIELDS + layer, 1), :] = k_v[pl.ds(base, 1), :]
        hy_s[0, 1, pl.ds(FIELDS + layer, 1), :] = k_v[pl.ds(base + CY - 1, 1), :]

    pl.semaphore_wait(barrier, DEVICES - 1)
    first_halo = halo_copies(0)
    for copy in first_halo:
        copy.start()

    def beside_x(edges, q, lane, west, east):
        turned = pltpu.roll(edges, CX - 1 - 2 * q, axis=1)
        return jnp.where(lane == 0, turned, west), jnp.where(lane == CX - 1, turned, east)

    def make_weights(layer, carry):
        base = pl.multiple_of((layer + 1) * PAD, 8)
        centre = k_v[pl.ds(base + 8, CY), :]
        west, east = beside_x(
            hx_r[0, 0],
            FIELDS + layer,
            lane_y,
            pltpu.roll(centre, 1, axis=1),
            pltpu.roll(centre, CX - 1, axis=1),
        )
        others = (
            k_v[pl.ds(base + 8 + PAD, CY), :],
            k_v[pl.ds(base + 8 - PAD, CY), :],
            k_v[pl.ds(base + 9, CY), :],
            k_v[pl.ds(base + 7, CY), :],
            east,
            west,
        )
        for i, other in enumerate(others):
            t_v[i, field(layer), :] = 2.0 * centre * other / (centre + other)
        return carry

    lane_r = lax.broadcasted_iota(jnp.int32, (ROWS, CX), 1)

    def part_rows(layer, c, r0):
        return pl.ds(pl.multiple_of((layer * NC + c) * CY + r0, ROWS), ROWS)

    def diag_pass(layer, source, held):
        for r0 in range(0, CY, ROWS):
            well = mask_v[pl.ds(r0, ROWS), :].astype(F32)
            acc = [well * source[part_rows(layer, c, r0), :] for c in range(NC)]
            for r in range(NC):
                base = pl.multiple_of((layer + 1) * (NC * PAD) + (r * PAD + 8 + r0), 8)
                own = w_v[pl.ds(base, ROWS), :]
                west_v[part_rows(layer, r, r0), :] = pltpu.roll(own, 1, axis=1)
                east_v[part_rows(layer, r, r0), :] = pltpu.roll(own, CX - 1, axis=1)
                for c in range(NC):
                    acc[c] = acc[c] + diag_v[layer, r, c, pl.ds(r0, ROWS), :].astype(F32) * own
            for c in range(NC):
                held[part_rows(layer, c, r0), :] = acc[c]

    def flux_pass(layer, which, held, put):
        for r0 in range(0, CY, ROWS):
            rows = pl.ds(pl.multiple_of(layer * CY + r0, ROWS), ROWS)
            weights = [t_v[i, rows, :] for i in range(6)]
            edges = hx_r[which, 0, pl.ds(r0, ROWS), :]
            acc = [held[part_rows(layer, c, r0), :] for c in range(NC)]
            for r in range(NC):
                base = pl.multiple_of((layer + 1) * (NC * PAD) + (r * PAD + 8 + r0), 8)
                here = part_rows(layer, r, r0)
                west, east = beside_x(
                    edges, layer * NC + r, lane_r, west_v[here, :], east_v[here, :]
                )
                total = weights[0] * w_v[pl.ds(base + NC * PAD, ROWS), :]
                total = total + weights[1] * w_v[pl.ds(base - NC * PAD, ROWS), :]
                total = total + weights[2] * w_v[pl.ds(base + 1, ROWS), :]
                total = total + weights[3] * w_v[pl.ds(base - 1, ROWS), :]
                total = total + weights[4] * east
                total = total + weights[5] * west
                for c in range(NC):
                    acc[c] = acc[c] - flux_v[layer, r, c, pl.ds(r0, ROWS), :].astype(F32) * total
            for c in range(NC):
                put(layer, c, r0, acc[c])

    def put_first(layer, c, r0, value):
        lanes = pl.ds(pl.multiple_of(layer * CX, CX), CX)
        f16_v[pl.ds(c * CY + r0, ROWS), lanes] = value.astype(BF16)
        s2_v[part_rows(layer, c, r0), :] = value

    def first_diag(layer, carry):
        block_copy(0, layer).wait()
        diag_pass(layer, cot_v, s2_v)
        return carry

    def first_flux(layer, carry):
        block_copy(1, layer).wait()
        flux_pass(layer, 0, s2_v, put_first)
        return carry

    lax.fori_loop(0, LAYERS, first_diag, 0)

    for copy in table_loads:
        copy.wait()
    lane_i = lax.broadcasted_iota(jnp.int32, (BLOCKS, BLK), 1)
    row_i = lax.broadcasted_iota(jnp.int32, (BLOCKS, BLK), 0)
    target = lax.rem(row_i + me + 1, DEVICES)
    choose = jnp.where(helper_ref[...] == target, 1.0, 0.0).astype(BF16)
    cells = cells_ref[...]
    cell_layer = lax.shift_right_logical(cells, 13).astype(F32).astype(BF16)
    cell_y = lax.shift_right_logical(cells, 7) & (CY - 1)
    cell_y = jnp.where(row_i < count_ref[0, 0], cell_y, CY).astype(F32).astype(BF16)
    cell_x = (cells & (CX - 1)).astype(F32).astype(BF16)
    code_v[...] = CX * jnp.dot(choose, cell_layer, preferred_element_type=F32) + jnp.dot(
        choose, cell_x, preferred_element_type=F32
    )
    y_v[...] = jnp.dot(choose, cell_y, preferred_element_type=F32)

    for copy in first_halo:
        copy.wait_recv()
    edge_columns(0)
    edge_rows(0)
    for layer in range(LAYERS):
        base = (layer + 1) * PAD
        k_v[pl.ds(base + 7, 1), :] = jnp.where(gy > 0, hy_r[0, 0, pl.ds(FIELDS + layer, 1), :], 0.0)
        k_v[pl.ds(base + 8 + CY, 1), :] = jnp.where(
            gy < WY - 1, hy_r[0, 1, pl.ds(FIELDS + layer, 1), :], 0.0
        )
    lax.fori_loop(0, LAYERS, make_weights, 0)
    lax.fori_loop(0, LAYERS, first_flux, 0)
    for copy in flash_loads:
        copy.wait()

    iota_x = lax.broadcasted_iota(jnp.int32, (CX, BLK), 0).astype(F32).astype(BF16)
    iota_y = lax.broadcasted_iota(jnp.int32, (CY, BLK), 0).astype(F32)
    iota_y16 = iota_y.astype(BF16)
    one16 = jnp.ones((CX, BLK), BF16)
    zero16 = jnp.zeros((CX, BLK), BF16)

    def one_hot(chunk, b):
        code = code_v[pl.ds(chunk * NB + b, 1), :]
        for layer in range(LAYERS):
            own_x = jnp.broadcast_to((code - float(layer * CX)).astype(BF16), (CX, BLK))
            oh_v[chunk, pl.ds(layer * CX, CX), pl.ds(b * BLK, BLK)] = jnp.where(
                own_x == iota_x, one16, zero16
            )

    def send_chunk(buf, to, chunk, sign, send, recv):
        for b in range(NB):
            p = chunk * NB + b

            def remote():
                pltpu.make_async_remote_copy(
                    src_ref=buf.at[p],
                    dst_ref=to.at[p],
                    send_sem=send.at[chunk],
                    recv_sem=recv.at[chunk],
                    device_id=device(lax.rem(me + sign * (p + 1) + DEVICES, DEVICES)),
                    device_id_type=MESH,
                ).start()

            if b < NB - 1:
                remote()
            else:
                pl.when(chunk < CHUNKS - 1)(remote)

                @pl.when(chunk == CHUNKS - 1)
                def _():
                    pltpu.make_async_copy(buf.at[p], to.at[p], recv.at[chunk]).start()

    def chunk_copy(buf, to, chunk, count, send, recv):
        rows = pl.ds(chunk * NB, count)
        return pltpu.make_async_remote_copy(
            src_ref=buf.at[rows],
            dst_ref=to.at[rows],
            send_sem=send.at[chunk],
            recv_sem=recv.at[chunk],
            device_id=device(lax.rem(me + 1, DEVICES)),
            device_id_type=MESH,
        )

    def gather(chunk):
        for first in range(0, NB, SUB):
            for b in range(first, first + SUB):
                one_hot(chunk, b)
            wide = jnp.dot(
                f16_v[...],
                oh_v[chunk, :, first * BLK : (first + SUB) * BLK],
                preferred_element_type=F32,
            )
            for b in range(SUB):
                p = chunk * NB + first + b
                hit = jnp.broadcast_to(y_v[pl.ds(p, 1), :], (CY, BLK)) == iota_y
                found = []
                for c in range(NC):
                    piece = wide[c * CY : (c + 1) * CY, b * BLK : (b + 1) * BLK]
                    found.append(jnp.sum(jnp.where(hit, piece, 0.0), axis=0, keepdims=True))
                ps[p] = jnp.concatenate(found, axis=0).astype(BF16)

    def flash(chunk):
        total = g_v[...]
        for b in range(NB):
            p = chunk * NB + b
            source = lax.rem(me - (p + 1) + DEVICES, DEVICES)
            chosen = rb[p].astype(F32)
            multiplier = jnp.sum(inv_v[source].astype(F32) * chosen[:, None, :], axis=0)
            change = -jnp.sum(coup_v[source].astype(F32) * multiplier[:, None, :], axis=0)
            state = phase_v[source].astype(F32)
            total = total + (multiplier * state)[None] * state[:, None, :]
            cs[p] = change.astype(BF16)
        g_v[...] = total

    def scatter(chunk):
        for b in range(NB):
            p = chunk * NB + b
            hit = jnp.broadcast_to(y_v[pl.ds(p, 1), :].astype(BF16), (CY, BLK)) == iota_y16
            change = cr[p]
            for c in range(NC):
                lhs_v[pl.ds(c * CY, CY), pl.ds(b * BLK, BLK)] = jnp.where(
                    hit, jnp.broadcast_to(change[c : c + 1], (CY, BLK)), zero16[:CY]
                )
        added = lax.dot_general(
            lhs_v[...], oh_v[chunk], (((1,), (1,)), ((), ())), preferred_element_type=F32
        )
        for layer in range(LAYERS):
            rows = pl.ds(layer * NC * CY, NC * CY)
            s2_v[rows, :] = s2_v[rows, :] + added[:, layer * CX : (layer + 1) * CX]

    g_v[...] = jnp.zeros_like(g_v)

    def loop(low, high, gathers=None, flashes=None, scatters=None):
        def body(t, carry):
            if flashes is not None:
                chunk_copy(ps, rb, t - flashes, NB, ps_send, ps_recv).wait_recv()
            if scatters is not None:
                chunk_copy(cs, cr, t - scatters, NB, cs_send, cs_recv).wait_recv()
            if gathers is not None:
                gather(t - gathers)
            if flashes is not None:
                flash(t - flashes)
            if scatters is not None:
                scatter(t - scatters)
            if gathers is not None:
                send_chunk(ps, rb, t - gathers, 1, ps_send, ps_recv)
            if flashes is not None:
                send_chunk(cs, cr, t - flashes, -1, cs_send, cs_recv)
            return carry

        lax.fori_loop(low, high, body, 0)

    loop(0, DELAY, gathers=0)
    loop(DELAY, CHUNKS, gathers=0, flashes=DELAY)
    loop(CHUNKS, CHUNKS + DELAY, flashes=DELAY, scatters=CHUNKS)

    lane_g = lax.broadcasted_iota(jnp.int32, (NC, CX), 1)
    tile = jnp.zeros((NC, CX), F32)
    for j in range(NC):
        tile = jnp.where(lane_g == j, jnp.sum(g_v[j], axis=1, keepdims=True), tile)
    gt[...] = tile
    ga[gx] = tile

    def grad_copy(source, target_ref, where, phase):
        return pltpu.make_async_remote_copy(
            src_ref=source,
            dst_ref=target_ref,
            send_sem=g_send.at[phase],
            recv_sem=g_recv.at[phase],
            device_id=where,
            device_id_type=MESH,
        )

    def send_x(step, carry):
        grad_copy(gt, ga.at[gx], (lax.rem(gx + step, WX), gy), 0).start()
        return carry

    lax.fori_loop(1, WX, send_x, 0)

    loop(CHUNKS + DELAY, 2 * CHUNKS, scatters=CHUNKS)

    some = ga.at[pl.ds(0, WX - 1)]
    grad_copy(some, some, (lax.rem(gx + 1, WX), gy), 0).wait_recv()
    part = ga[0]
    for i in range(1, WX):
        part = part + ga[i]
    gt2[...] = part
    gb[gy] = part

    def send_y(step, carry):
        grad_copy(gt2, gb.at[gy], (gx, lax.rem(gy + step, WY)), 1).start()
        return carry

    lax.fori_loop(1, WY, send_y, 0)

    mask_fields(s2_v, 1, (zero_edge, zero_edge))
    second_halo = halo_copies(1)
    for copy in second_halo:
        copy.start()

    def second_diag(layer, carry):
        diag_pass(layer, s2_v, out_v)
        return carry

    lax.fori_loop(0, LAYERS, second_diag, 0)
    for copy in second_halo:
        copy.wait_recv()
    edge_columns(1)
    edge_rows(1)

    def put_second(layer, c, r0, value):
        out_v[part_rows(layer, c, r0), :] = value

    def second_flux(layer, carry):
        flux_pass(layer, 1, out_v, put_second)
        return carry

    lax.fori_loop(0, LAYERS, second_flux, 0)

    some = gb.at[pl.ds(0, WY - 1)]
    grad_copy(some, some, (gx, lax.rem(gy + 1, WY)), 1).wait_recv()
    total = gb[0]
    for i in range(1, WY):
        total = total + gb[i]
    scale = -1.0 / math.sqrt(BLK * BLOCKS * DEVICES)
    grad_ref[...] = scale * total[:, :NC]

    for copy in first_halo + second_halo:
        copy.wait_send()
    some = ga.at[pl.ds(0, WX - 1)]
    grad_copy(some, some, (lax.rem(gx + 1, WX), gy), 0).wait_send()
    some = gb.at[pl.ds(0, WY - 1)]
    grad_copy(some, some, (gx, lax.rem(gy + 1, WY)), 1).wait_send()

    def drain(chunk, carry):
        chunk_copy(ps, rb, chunk, NB, ps_send, ps_recv).wait_send()
        chunk_copy(cs, cr, chunk, NB, cs_send, cs_recv).wait_send()
        return carry

    lax.fori_loop(0, CHUNKS - 1, drain, 0)
    chunk_copy(ps, rb, CHUNKS - 1, NB - 1, ps_send, ps_recv).wait_send()
    chunk_copy(cs, cr, CHUNKS - 1, NB - 1, cs_send, cs_recv).wait_send()


def shards(
    cotangent, permeability, well_mask, diag_block, flux_block, cell_list, block_count, helper_of,
    flash_inverse, flash_coupling, phase_state,
):
    hbm = pl.BlockSpec(memory_space=pltpu.HBM)
    smem = pl.BlockSpec(memory_space=pltpu.SMEM)
    vmem = pl.BlockSpec(memory_space=pltpu.VMEM)
    dma = pltpu.SemaphoreType.DMA
    def pin(array):
        return pltpu.with_memory_space_constraint(array, pltpu.HBM)

    adjoint, grad = pl.pallas_call(
        kernel,
        out_shape=(
            pltpu.VMEM((FIELDS * CY, CX), F32),
            pltpu.VMEM((NC, NC), F32),
        ),
        in_specs=[hbm] * 6 + [smem] + [hbm] * 4,
        out_specs=(vmem, vmem),
        scratch_shapes=[
            pltpu.VMEM((FIELDS * CY, CX), F32),
            pltpu.VMEM((LAYERS * CY, CX), F32),
            pltpu.VMEM((CY, CX), jnp.int32),
            pltpu.VMEM((BLOCKS, BLK), jnp.int32),
            pltpu.VMEM((1, BLOCKS), jnp.int32),
            pltpu.VMEM((LAYERS, NC, NC, CY, CX), BF16),
            pltpu.VMEM((LAYERS, NC, NC, CY, CX), BF16),
            pltpu.VMEM((BLOCKS, NC, NC, BLK), BF16),
            pltpu.VMEM((BLOCKS, NC, NC, BLK), BF16),
            pltpu.VMEM((BLOCKS, NC, BLK), BF16),
            pltpu.VMEM(((FIELDS + 2 * NC) * PAD, CX), F32),
            pltpu.VMEM((FIELDS * CY, CX), F32),
            pltpu.VMEM((FIELDS * CY, CX), F32),
            pltpu.VMEM(((LAYERS + 2) * PAD, CX), F32),
            pltpu.VMEM((6, LAYERS * CY, CX), F32),
            pltpu.VMEM((NC * CY, LAYERS * CX), BF16),
            pltpu.VMEM((FIELDS * CY, CX), F32),
            pltpu.VMEM((BLOCKS, BLK), F32),
            pltpu.VMEM((BLOCKS, BLK), F32),
            pltpu.VMEM((CHUNKS, LAYERS * CX, NB * BLK), BF16),
            pltpu.VMEM((NC * CY, NB * BLK), BF16),
            pltpu.VMEM((BLOCKS, NC, BLK), BF16),
            pltpu.VMEM((BLOCKS, NC, BLK), BF16),
            pltpu.VMEM((BLOCKS, NC, BLK), BF16),
            pltpu.VMEM((BLOCKS, NC, BLK), BF16),
            pltpu.VMEM((NC, NC, BLK), F32),
            pltpu.VMEM((NC, CX), F32),
            pltpu.VMEM((WX, NC, CX), F32),
            pltpu.VMEM((NC, CX), F32),
            pltpu.VMEM((WY, NC, CX), F32),
            pltpu.VMEM((2, 2, CY, CX), F32),
            pltpu.VMEM((2, 2, CY, CX), F32),
            pltpu.VMEM((2, 2, 56, CX), F32),
            pltpu.VMEM((2, 2, 56, CX), F32),
            dma((5,)),
            dma((2, LAYERS)),
            dma((3,)),
            dma((2, 4)),
            dma((2, 4)),
            dma((CHUNKS,)),
            dma((CHUNKS,)),
            dma((CHUNKS,)),
            dma((CHUNKS,)),
            dma((2,)),
            dma((2,)),
        ],
        compiler_params=pltpu.CompilerParams(
            collective_id=0, has_side_effects=True, vmem_limit_bytes=60 << 20
        ),
    )(
        pin(cotangent.reshape(FIELDS * CY, CX)),
        pin(permeability.reshape(LAYERS * CY, CX)),
        pin(well_mask),
        pin(diag_block),
        pin(flux_block),
        pin(cell_list.reshape(BLOCKS, BLK)),
        block_count,
        pin(helper_of.reshape(1, BLOCKS)),
        pin(flash_inverse.reshape(BLOCKS, NC, NC, BLK)),
        pin(flash_coupling.reshape(BLOCKS, NC, NC, BLK)),
        pin(phase_state.reshape(BLOCKS, NC, BLK)),
    )
    return adjoint.reshape(cotangent.shape), grad


def solution(mesh):
    return jax.shard_map(
        shards,
        mesh=mesh,
        in_specs=(
            P(None, None, "gy", "gx"),
            P(None, "gy", "gx"),
            P("gy", "gx"),
            P(None, None, None, "gy", "gx"),
            P(None, None, None, "gy", "gx"),
            P("gy", "gx", None),
            P("gy", "gx"),
            P("gy", "gx", None),
            P("gy", "gx", None, None, None, None),
            P("gy", "gx", None, None, None, None),
            P("gy", "gx", None, None, None),
        ),
        out_specs=(P(None, None, "gy", "gx"), P()),
        check_vma=False,
    )
```

```python
import functools
import math

import jax
import jax.numpy as jnp
from jax import lax
from jax.experimental import pallas as pl
from jax.experimental.pallas import tpu as pltpu
from jax.sharding import PartitionSpec as P

MESH = pl.DeviceIdType.MESH
F32 = jnp.float32
BF16 = jnp.bfloat16

LAYERS, NC, CY, CX = 6, 8, 64, 128
FIELDS = LAYERS * NC
PAD = 80
WX, WY = 8, 16
DEVICES = WX * WY
BLOCKS, BLK = 128, 128
NB = 16
SUB = 8
CHUNKS = BLOCKS // NB
DELAY = 4
ROWS = 16


def kernel(
    cot_h, perm_h, mask_h, diag_h, flux_h, cells_h, count_ref, helper_h, inv_h, coup_h, phase_h,
    out_v, grad_ref,
    cot_v, perm_v, mask_v, cells_ref, helper_ref, diag_v, flux_v, inv_v, coup_v, phase_v,
    w_v, west_v, east_v, k_v, t_v, f16_v, s2_v, code_v, y_v, oh_v, lhs_v,
    ps, rb, cs, cr, row_v, g_v, gt, ga, gt2, gb,
    hx_s, hx_r, hy_s, hy_r,
    load_sem, cot_sem, blk_sem, fl_sem,
    halo_send, halo_recv, ps_send, ps_recv, cs_send, cs_recv, g_send, g_recv,
):
    gx = lax.axis_index("gx")
    gy = lax.axis_index("gy")
    me = gx * WY + gy

    def device(linear):
        return (lax.div(linear, WY), lax.rem(linear, WY))

    def cot_copy(layer):
        rows = pl.ds(pl.multiple_of(layer * NC * CY, NC * CY), NC * CY)
        return pltpu.make_async_copy(cot_h.at[rows], cot_v.at[rows], cot_sem.at[layer])

    loads = [
        pltpu.make_async_copy(perm_h, perm_v, load_sem.at[1]),
        pltpu.make_async_copy(mask_h, mask_v, load_sem.at[2]),
    ]
    table_loads = [
        pltpu.make_async_copy(cells_h, cells_ref, load_sem.at[3]),
        pltpu.make_async_copy(helper_h, helper_ref, load_sem.at[4]),
    ]
    for copy in loads:
        copy.start()
    for layer in range(LAYERS):
        cot_copy(layer).start()

    barrier = pltpu.get_barrier_semaphore()

    def greet(step, carry):
        pl.semaphore_signal(
            barrier, inc=1, device_id=device(lax.rem(me + step, DEVICES)), device_id_type=MESH
        )
        return carry

    lax.fori_loop(1, DEVICES, greet, 0)

    for copy in table_loads:
        copy.start()

    def block_copy(which, layer):
        source, held = ((diag_h, diag_v), (flux_h, flux_v))[which]
        return pltpu.make_async_copy(source.at[layer], held.at[layer], blk_sem.at[which, layer])

    for which in range(2):
        for layer in range(LAYERS):
            block_copy(which, layer).start()
    flash_loads = [
        pltpu.make_async_copy(inv_h, inv_v, fl_sem.at[0]),
        pltpu.make_async_copy(coup_h, coup_v, fl_sem.at[1]),
        pltpu.make_async_copy(phase_h, phase_v, fl_sem.at[2]),
    ]
    for copy in flash_loads:
        copy.start()

    w_v[pl.ds(0, NC * PAD), :] = jnp.zeros((NC * PAD, CX), F32)
    w_v[pl.ds((FIELDS + NC) * PAD, NC * PAD), :] = jnp.zeros((NC * PAD, CX), F32)
    k_v[pl.ds(0, PAD), :] = jnp.zeros((PAD, CX), F32)
    k_v[pl.ds((LAYERS + 1) * PAD, PAD), :] = jnp.zeros((PAD, CX), F32)

    for copy in loads:
        copy.wait()

    lane_y = lax.broadcasted_iota(jnp.int32, (CY, CX), 1)
    hole = mask_v[...].astype(F32)
    keep = 1.0 - hole

    def field(q):
        return pl.ds(pl.multiple_of(q * CY, CY), CY)

    def pack_edges(q, value, carry):
        right, left = carry
        turned = pltpu.roll(value, 2 * q + 2, axis=1)
        right = jnp.where(lane_y == 2 * q + 1, turned, right)
        left = jnp.where(lane_y == 2 * q + 2, turned, left)
        return right, left

    def mask_fields(source, which, start):
        def step(layer, carry):
            if which == 0:
                cot_copy(layer).wait()
            for c in range(NC):
                q = layer * NC + c
                value = source[field(q), :] * keep
                w_v[pl.ds(pl.multiple_of((q + NC) * PAD + 8, 8), CY), :] = value
                carry = pack_edges(q, value, carry)
            return carry

        right, left = lax.fori_loop(0, LAYERS, step, start)
        hx_s[which, 0] = pltpu.roll(left, CX - 2, axis=1)
        hx_s[which, 1] = right
        for layer in range(LAYERS):
            base = (layer + 1) * NC * PAD + 8
            hy_s[which, 0, pl.ds(layer * NC, NC), :] = w_v[pl.ds(base, NC, stride=PAD), :]
            hy_s[which, 1, pl.ds(layer * NC, NC), :] = w_v[pl.ds(base + CY - 1, NC, stride=PAD), :]

    def halo_copies(which):
        east = (lax.rem(gx + 1, WX), gy)
        west = (lax.rem(gx + WX - 1, WX), gy)
        south = (gx, lax.rem(gy + 1, WY))
        north = (gx, lax.rem(gy + WY - 1, WY))
        plan = (
            (hx_s.at[which, 1], hx_r.at[which, 0], east),
            (hx_s.at[which, 0], hx_r.at[which, 1], west),
            (hy_s.at[which, 1], hy_r.at[which, 0], south),
            (hy_s.at[which, 0], hy_r.at[which, 1], north),
        )
        return [
            pltpu.make_async_remote_copy(
                src_ref=source,
                dst_ref=target_ref,
                send_sem=halo_send.at[which, i],
                recv_sem=halo_recv.at[which, i],
                device_id=where,
                device_id_type=MESH,
            )
            for i, (source, target_ref, where) in enumerate(plan)
        ]

    def edge_columns(which):
        odd = lax.rem(lane_y, 2) == 1
        from_west = jnp.where(gx > 0, hx_r[which, 0], 0.0)
        from_east = jnp.where(gx < WX - 1, hx_r[which, 1], 0.0)
        hx_r[which, 0] = jnp.where(odd, from_west, from_east)

    def edge_rows(which):
        for layer in range(LAYERS):
            base = (layer + 1) * NC * PAD
            rows = pl.ds(layer * NC, NC)
            w_v[pl.ds(base + 7, NC, stride=PAD), :] = jnp.where(gy > 0, hy_r[which, 0, rows, :], 0.0)
            w_v[pl.ds(base + 8 + CY, NC, stride=PAD), :] = jnp.where(
                gy < WY - 1, hy_r[which, 1, rows, :], 0.0
            )

    zero_edge = jnp.zeros((CY, CX), F32)
    start = (zero_edge, zero_edge)
    for layer in range(LAYERS):
        value = perm_v[pl.ds(layer * CY, CY), :]
        k_v[pl.ds((layer + 1) * PAD + 8, CY), :] = value
        start = pack_edges(FIELDS + layer, value, start)
    mask_fields(cot_v, 0, start)
    for layer in range(LAYERS):
        base = (layer + 1) * PAD + 8
        hy_s[0, 0, pl.ds(FIELDS + layer, 1), :] = k_v[pl.ds(base, 1), :]
        hy_s[0, 1, pl.ds(FIELDS + layer, 1), :] = k_v[pl.ds(base + CY - 1, 1), :]

    pl.semaphore_wait(barrier, DEVICES - 1)
    first_halo = halo_copies(0)
    for copy in first_halo:
        copy.start()

    def beside_x(edges, q, lane, west, east):
        turned = pltpu.roll(edges, CX - 1 - 2 * q, axis=1)
        return jnp.where(lane == 0, turned, west), jnp.where(lane == CX - 1, turned, east)

    def make_weights(layer, carry):
        base = pl.multiple_of((layer + 1) * PAD, 8)
        centre = k_v[pl.ds(base + 8, CY), :]
        west, east = beside_x(
            hx_r[0, 0],
            FIELDS + layer,
            lane_y,
            pltpu.roll(centre, 1, axis=1),
            pltpu.roll(centre, CX - 1, axis=1),
        )
        others = (
            k_v[pl.ds(base + 8 + PAD, CY), :],
            k_v[pl.ds(base + 8 - PAD, CY), :],
            k_v[pl.ds(base + 9, CY), :],
            k_v[pl.ds(base + 7, CY), :],
            east,
            west,
        )
        for i, other in enumerate(others):
            t_v[i, field(layer), :] = 2.0 * centre * other / (centre + other)
        return carry

    lane_r = lax.broadcasted_iota(jnp.int32, (ROWS, CX), 1)

    def part_rows(layer, c, r0):
        return pl.ds(pl.multiple_of((layer * NC + c) * CY + r0, ROWS), ROWS)

    def diag_pass(layer, source, held):
        for r0 in range(0, CY, ROWS):
            well = mask_v[pl.ds(r0, ROWS), :].astype(F32)
            acc = [well * source[part_rows(layer, c, r0), :] for c in range(NC)]
            for r in range(NC):
                base = pl.multiple_of((layer + 1) * (NC * PAD) + (r * PAD + 8 + r0), 8)
                own = w_v[pl.ds(base, ROWS), :]
                west_v[part_rows(layer, r, r0), :] = pltpu.roll(own, 1, axis=1)
                east_v[part_rows(layer, r, r0), :] = pltpu.roll(own, CX - 1, axis=1)
                for c in range(NC):
                    acc[c] = acc[c] + diag_v[layer, r, c, pl.ds(r0, ROWS), :].astype(F32) * own
            for c in range(NC):
                held[part_rows(layer, c, r0), :] = acc[c]

    def flux_pass(layer, which, held, put):
        for r0 in range(0, CY, ROWS):
            rows = pl.ds(pl.multiple_of(layer * CY + r0, ROWS), ROWS)
            weights = [t_v[i, rows, :] for i in range(6)]
            edges = hx_r[which, 0, pl.ds(r0, ROWS), :]
            acc = [held[part_rows(layer, c, r0), :] for c in range(NC)]
            for r in range(NC):
                base = pl.multiple_of((layer + 1) * (NC * PAD) + (r * PAD + 8 + r0), 8)
                here = part_rows(layer, r, r0)
                west, east = beside_x(
                    edges, layer * NC + r, lane_r, west_v[here, :], east_v[here, :]
                )
                total = weights[0] * w_v[pl.ds(base + NC * PAD, ROWS), :]
                total = total + weights[1] * w_v[pl.ds(base - NC * PAD, ROWS), :]
                total = total + weights[2] * w_v[pl.ds(base + 1, ROWS), :]
                total = total + weights[3] * w_v[pl.ds(base - 1, ROWS), :]
                total = total + weights[4] * east
                total = total + weights[5] * west
                for c in range(NC):
                    acc[c] = acc[c] - flux_v[layer, r, c, pl.ds(r0, ROWS), :].astype(F32) * total
            for c in range(NC):
                put(layer, c, r0, acc[c])

    def put_first(layer, c, r0, value):
        lanes = pl.ds(pl.multiple_of(layer * CX, CX), CX)
        f16_v[pl.ds(c * CY + r0, ROWS), lanes] = value.astype(BF16)
        s2_v[part_rows(layer, c, r0), :] = value

    def first_diag(layer, carry):
        block_copy(0, layer).wait()
        diag_pass(layer, cot_v, s2_v)
        return carry

    def first_flux(layer, carry):
        block_copy(1, layer).wait()
        flux_pass(layer, 0, s2_v, put_first)
        return carry

    lax.fori_loop(0, LAYERS, first_diag, 0)

    for copy in table_loads:
        copy.wait()
    lane_i = lax.broadcasted_iota(jnp.int32, (BLOCKS, BLK), 1)
    row_i = lax.broadcasted_iota(jnp.int32, (BLOCKS, BLK), 0)
    target = lax.rem(row_i + me + 1, DEVICES)
    choose = jnp.where(helper_ref[...] == target, 1.0, 0.0).astype(BF16)
    cells = cells_ref[...]
    cell_layer = lax.shift_right_logical(cells, 13).astype(F32).astype(BF16)
    cell_y = lax.shift_right_logical(cells, 7) & (CY - 1)
    cell_y = jnp.where(row_i < count_ref[0, 0], cell_y, CY).astype(F32).astype(BF16)
    cell_x = (cells & (CX - 1)).astype(F32).astype(BF16)
    code_v[...] = CX * jnp.dot(choose, cell_layer, preferred_element_type=F32) + jnp.dot(
        choose, cell_x, preferred_element_type=F32
    )
    y_v[...] = jnp.dot(choose, cell_y, preferred_element_type=F32)

    for copy in first_halo:
        copy.wait_recv()
    edge_columns(0)
    edge_rows(0)
    for layer in range(LAYERS):
        base = (layer + 1) * PAD
        k_v[pl.ds(base + 7, 1), :] = jnp.where(gy > 0, hy_r[0, 0, pl.ds(FIELDS + layer, 1), :], 0.0)
        k_v[pl.ds(base + 8 + CY, 1), :] = jnp.where(
            gy < WY - 1, hy_r[0, 1, pl.ds(FIELDS + layer, 1), :], 0.0
        )
    lax.fori_loop(0, LAYERS, make_weights, 0)
    lax.fori_loop(0, LAYERS, first_flux, 0)
    for copy in flash_loads:
        copy.wait()

    iota_x = lax.broadcasted_iota(jnp.int32, (CX, BLK), 0).astype(F32).astype(BF16)
    iota_y = lax.broadcasted_iota(jnp.int32, (CY, BLK), 0).astype(F32)
    iota_y16 = iota_y.astype(BF16)
    one16 = jnp.ones((CX, BLK), BF16)
    zero16 = jnp.zeros((CX, BLK), BF16)

    def one_hot(chunk, b):
        code = code_v[pl.ds(chunk * NB + b, 1), :]
        for layer in range(LAYERS):
            own_x = jnp.broadcast_to((code - float(layer * CX)).astype(BF16), (CX, BLK))
            oh_v[chunk, pl.ds(layer * CX, CX), pl.ds(b * BLK, BLK)] = jnp.where(
                own_x == iota_x, one16, zero16
            )

    def send_chunk(buf, to, chunk, sign, send, recv):
        for b in range(NB):
            p = chunk * NB + b

            def remote():
                pltpu.make_async_remote_copy(
                    src_ref=buf.at[p],
                    dst_ref=to.at[p],
                    send_sem=send.at[chunk],
                    recv_sem=recv.at[chunk],
                    device_id=device(lax.rem(me + sign * (p + 1) + DEVICES, DEVICES)),
                    device_id_type=MESH,
                ).start()

            if b < NB - 1:
                remote()
            else:
                pl.when(chunk < CHUNKS - 1)(remote)

                @pl.when(chunk == CHUNKS - 1)
                def _():
                    pltpu.make_async_copy(buf.at[p], to.at[p], recv.at[chunk]).start()

    def chunk_copy(buf, to, chunk, count, send, recv):
        rows = pl.ds(chunk * NB, count)
        return pltpu.make_async_remote_copy(
            src_ref=buf.at[rows],
            dst_ref=to.at[rows],
            send_sem=send.at[chunk],
            recv_sem=recv.at[chunk],
            device_id=device(lax.rem(me + 1, DEVICES)),
            device_id_type=MESH,
        )

    def gather(chunk):
        for first in range(0, NB, SUB):
            for b in range(first, first + SUB):
                one_hot(chunk, b)
            wide = jnp.dot(
                f16_v[...],
                oh_v[chunk, :, first * BLK : (first + SUB) * BLK],
                preferred_element_type=F32,
            )
            for b in range(SUB):
                p = chunk * NB + first + b
                hit = jnp.broadcast_to(y_v[pl.ds(p, 1), :], (CY, BLK)) == iota_y
                found = []
                for c in range(NC):
                    piece = wide[c * CY : (c + 1) * CY, b * BLK : (b + 1) * BLK]
                    found.append(jnp.sum(jnp.where(hit, piece, 0.0), axis=0, keepdims=True))
                ps[p] = jnp.concatenate(found, axis=0).astype(BF16)

    def spread(value, b, i):
        row_v[b, i] = value
        return [jnp.broadcast_to(row_v[b, i, pl.ds(r, 1), :], (NC, BLK)) for r in range(NC)]

    def weighted(matrix, rows):
        total = matrix[0] * rows[0]
        for r in range(1, NC):
            total = total + matrix[r] * rows[r]
        return total

    def flash(chunk):
        totals = [g_v[j] for j in range(NC)]
        for b in range(NB):
            p = chunk * NB + b
            source = lax.rem(me - (p + 1) + DEVICES, DEVICES)
            multiplier = weighted(inv_v[source].astype(F32), spread(rb[p].astype(F32), b, 0))
            change = -weighted(coup_v[source].astype(F32), spread(multiplier, b, 1))
            cs[p] = change.astype(BF16)
            state = phase_v[source].astype(F32)
            term = multiplier * state
            for j, row in enumerate(spread(state, b, 2)):
                totals[j] = totals[j] + term * row
        for j in range(NC):
            g_v[j] = totals[j]

    def scatter(chunk):
        for b in range(NB):
            p = chunk * NB + b
            hit = jnp.broadcast_to(y_v[pl.ds(p, 1), :].astype(BF16), (CY, BLK)) == iota_y16
            change = cr[p]
            for c in range(NC):
                lhs_v[pl.ds(c * CY, CY), pl.ds(b * BLK, BLK)] = jnp.where(
                    hit, jnp.broadcast_to(change[c : c + 1], (CY, BLK)), zero16[:CY]
                )
        added = lax.dot_general(
            lhs_v[...], oh_v[chunk], (((1,), (1,)), ((), ())), preferred_element_type=F32
        )
        for layer in range(LAYERS):
            rows = pl.ds(layer * NC * CY, NC * CY)
            s2_v[rows, :] = s2_v[rows, :] + added[:, layer * CX : (layer + 1) * CX]

    g_v[...] = jnp.zeros_like(g_v)

    def loop(low, high, gathers=None, flashes=None, scatters=None):
        def body(t, carry):
            if flashes is not None:
                chunk_copy(ps, rb, t - flashes, NB, ps_send, ps_recv).wait_recv()
            if scatters is not None:
                chunk_copy(cs, cr, t - scatters, NB, cs_send, cs_recv).wait_recv()
            if gathers is not None:
                gather(t - gathers)
            if flashes is not None:
                flash(t - flashes)
            if scatters is not None:
                scatter(t - scatters)
            if gathers is not None:
                send_chunk(ps, rb, t - gathers, 1, ps_send, ps_recv)
            if flashes is not None:
                send_chunk(cs, cr, t - flashes, -1, cs_send, cs_recv)
            return carry

        lax.fori_loop(low, high, body, 0)

    loop(0, DELAY, gathers=0)
    loop(DELAY, CHUNKS, gathers=0, flashes=DELAY)
    loop(CHUNKS, CHUNKS + DELAY, flashes=DELAY, scatters=CHUNKS)

    lane_g = lax.broadcasted_iota(jnp.int32, (NC, CX), 1)
    tile = jnp.zeros((NC, CX), F32)
    for j in range(NC):
        tile = jnp.where(lane_g == j, jnp.sum(g_v[j], axis=1, keepdims=True), tile)
    gt[...] = tile
    ga[gx] = tile

    def grad_copy(source, target_ref, where, phase):
        return pltpu.make_async_remote_copy(
            src_ref=source,
            dst_ref=target_ref,
            send_sem=g_send.at[phase],
            recv_sem=g_recv.at[phase],
            device_id=where,
            device_id_type=MESH,
        )

    def send_x(step, carry):
        grad_copy(gt, ga.at[gx], (lax.rem(gx + step, WX), gy), 0).start()
        return carry

    lax.fori_loop(1, WX, send_x, 0)

    loop(CHUNKS + DELAY, 2 * CHUNKS, scatters=CHUNKS)

    mask_fields(s2_v, 1, (zero_edge, zero_edge))
    second_halo = halo_copies(1)
    for copy in second_halo:
        copy.start()

    some = ga.at[pl.ds(0, WX - 1)]
    grad_copy(some, some, (lax.rem(gx + 1, WX), gy), 0).wait_recv()
    part = ga[0]
    for i in range(1, WX):
        part = part + ga[i]
    gt2[...] = part
    gb[gy] = part

    def send_y(step, carry):
        grad_copy(gt2, gb.at[gy], (gx, lax.rem(gy + step, WY)), 1).start()
        return carry

    lax.fori_loop(1, WY, send_y, 0)


    def second_diag(layer, carry):
        diag_pass(layer, s2_v, out_v)
        return carry

    lax.fori_loop(0, LAYERS, second_diag, 0)
    for copy in second_halo:
        copy.wait_recv()
    edge_columns(1)
    edge_rows(1)

    def put_second(layer, c, r0, value):
        out_v[part_rows(layer, c, r0), :] = value

    def second_flux(layer, carry):
        flux_pass(layer, 1, out_v, put_second)
        return carry

    lax.fori_loop(0, LAYERS, second_flux, 0)

    some = gb.at[pl.ds(0, WY - 1)]
    grad_copy(some, some, (gx, lax.rem(gy + 1, WY)), 1).wait_recv()
    total = gb[0]
    for i in range(1, WY):
        total = total + gb[i]
    scale = -1.0 / math.sqrt(BLK * BLOCKS * DEVICES)
    grad_ref[...] = scale * total[:, :NC]

    for copy in first_halo + second_halo:
        copy.wait_send()
    some = ga.at[pl.ds(0, WX - 1)]
    grad_copy(some, some, (lax.rem(gx + 1, WX), gy), 0).wait_send()
    some = gb.at[pl.ds(0, WY - 1)]
    grad_copy(some, some, (gx, lax.rem(gy + 1, WY)), 1).wait_send()

    def drain(chunk, carry):
        chunk_copy(ps, rb, chunk, NB, ps_send, ps_recv).wait_send()
        chunk_copy(cs, cr, chunk, NB, cs_send, cs_recv).wait_send()
        return carry

    lax.fori_loop(0, CHUNKS - 1, drain, 0)
    chunk_copy(ps, rb, CHUNKS - 1, NB - 1, ps_send, ps_recv).wait_send()
    chunk_copy(cs, cr, CHUNKS - 1, NB - 1, cs_send, cs_recv).wait_send()


def shards(
    cotangent, permeability, well_mask, diag_block, flux_block, cell_list, block_count, helper_of,
    flash_inverse, flash_coupling, phase_state,
):
    hbm = pl.BlockSpec(memory_space=pltpu.HBM)
    smem = pl.BlockSpec(memory_space=pltpu.SMEM)
    vmem = pl.BlockSpec(memory_space=pltpu.VMEM)
    dma = pltpu.SemaphoreType.DMA
    def pin(array):
        return pltpu.with_memory_space_constraint(array, pltpu.HBM)

    adjoint, grad = pl.pallas_call(
        kernel,
        out_shape=(
            pltpu.VMEM((FIELDS * CY, CX), F32),
            pltpu.VMEM((NC, NC), F32),
        ),
        in_specs=[hbm] * 6 + [smem] + [hbm] * 4,
        out_specs=(vmem, vmem),
        scratch_shapes=[
            pltpu.VMEM((FIELDS * CY, CX), F32),
            pltpu.VMEM((LAYERS * CY, CX), F32),
            pltpu.VMEM((CY, CX), jnp.int32),
            pltpu.VMEM((BLOCKS, BLK), jnp.int32),
            pltpu.VMEM((1, BLOCKS), jnp.int32),
            pltpu.VMEM((LAYERS, NC, NC, CY, CX), BF16),
            pltpu.VMEM((LAYERS, NC, NC, CY, CX), BF16),
            pltpu.VMEM((BLOCKS, NC, NC, BLK), BF16),
            pltpu.VMEM((BLOCKS, NC, NC, BLK), BF16),
            pltpu.VMEM((BLOCKS, NC, BLK), BF16),
            pltpu.VMEM(((FIELDS + 2 * NC) * PAD, CX), F32),
            pltpu.VMEM((FIELDS * CY, CX), F32),
            pltpu.VMEM((FIELDS * CY, CX), F32),
            pltpu.VMEM(((LAYERS + 2) * PAD, CX), F32),
            pltpu.VMEM((6, LAYERS * CY, CX), F32),
            pltpu.VMEM((NC * CY, LAYERS * CX), BF16),
            pltpu.VMEM((FIELDS * CY, CX), F32),
            pltpu.VMEM((BLOCKS, BLK), F32),
            pltpu.VMEM((BLOCKS, BLK), F32),
            pltpu.VMEM((CHUNKS, LAYERS * CX, NB * BLK), BF16),
            pltpu.VMEM((NC * CY, NB * BLK), BF16),
            pltpu.VMEM((BLOCKS, NC, BLK), BF16),
            pltpu.VMEM((BLOCKS, NC, BLK), BF16),
            pltpu.VMEM((BLOCKS, NC, BLK), BF16),
            pltpu.VMEM((BLOCKS, NC, BLK), BF16),
            pltpu.VMEM((NB, 3, NC, BLK), F32),
            pltpu.VMEM((NC, NC, BLK), F32),
            pltpu.VMEM((NC, CX), F32),
            pltpu.VMEM((WX, NC, CX), F32),
            pltpu.VMEM((NC, CX), F32),
            pltpu.VMEM((WY, NC, CX), F32),
            pltpu.VMEM((2, 2, CY, CX), F32),
            pltpu.VMEM((2, 2, CY, CX), F32),
            pltpu.VMEM((2, 2, 56, CX), F32),
            pltpu.VMEM((2, 2, 56, CX), F32),
            dma((5,)),
            dma((LAYERS,)),
            dma((2, LAYERS)),
            dma((3,)),
            dma((2, 4)),
            dma((2, 4)),
            dma((CHUNKS,)),
            dma((CHUNKS,)),
            dma((CHUNKS,)),
            dma((CHUNKS,)),
            dma((2,)),
            dma((2,)),
        ],
        compiler_params=pltpu.CompilerParams(
            collective_id=0, has_side_effects=True, vmem_limit_bytes=60 << 20
        ),
    )(
        pin(cotangent.reshape(FIELDS * CY, CX)),
        pin(permeability.reshape(LAYERS * CY, CX)),
        pin(well_mask),
        pin(diag_block),
        pin(flux_block),
        pin(cell_list.reshape(BLOCKS, BLK)),
        block_count,
        pin(helper_of.reshape(1, BLOCKS)),
        pin(flash_inverse.reshape(BLOCKS, NC, NC, BLK)),
        pin(flash_coupling.reshape(BLOCKS, NC, NC, BLK)),
        pin(phase_state.reshape(BLOCKS, NC, BLK)),
    )
    return adjoint.reshape(cotangent.shape), grad


def solution(mesh):
    return jax.shard_map(
        shards,
        mesh=mesh,
        in_specs=(
            P(None, None, "gy", "gx"),
            P(None, "gy", "gx"),
            P("gy", "gx"),
            P(None, None, None, "gy", "gx"),
            P(None, None, None, "gy", "gx"),
            P("gy", "gx", None),
            P("gy", "gx"),
            P("gy", "gx", None),
            P("gy", "gx", None, None, None, None),
            P("gy", "gx", None, None, None, None),
            P("gy", "gx", None, None, None),
        ),
        out_specs=(P(None, None, "gy", "gx"), P()),
        check_vma=False,
    )
```

```python
import functools
import math

import jax
import jax.numpy as jnp
from jax import lax
from jax.experimental import pallas as pl
from jax.experimental.pallas import tpu as pltpu
from jax.sharding import PartitionSpec as P

MESH = pl.DeviceIdType.MESH
F32 = jnp.float32
BF16 = jnp.bfloat16

LAYERS, NC, CY, CX = 6, 8, 64, 128
FIELDS = LAYERS * NC
PAD = 80
WX, WY = 8, 16
DEVICES = WX * WY
BLOCKS, BLK = 128, 128
NB = 16
SUB = 8
CHUNKS = BLOCKS // NB
DELAY = 4
ROWS = 16


def kernel(
    cot_h, perm_h, mask_h, diag_h, flux_h, cells_h, count_ref, helper_h, inv_h, coup_h, phase_h,
    out_v, grad_ref,
    cot_v, perm_v, mask_v, cells_ref, helper_ref, diag_v, flux_v, inv_v, coup_v, phase_v,
    w_v, west_v, east_v, k_v, t_v, f16_v, s2_v, code_v, y_v, oh_v, lhs_v,
    ps, rb, cs, cr, row_v, g_v, gt, ga, gt2, gb,
    hx_s, hx_r, hy_s, hy_r,
    load_sem, cot_sem, blk_sem, fl_sem,
    halo_send, halo_recv, ps_send, ps_recv, cs_send, cs_recv, g_send, g_recv,
):
    gx = lax.axis_index("gx")
    gy = lax.axis_index("gy")
    me = gx * WY + gy

    def device(linear):
        return (lax.div(linear, WY), lax.rem(linear, WY))

    def cot_copy(layer):
        rows = pl.ds(pl.multiple_of(layer * NC * CY, NC * CY), NC * CY)
        return pltpu.make_async_copy(cot_h.at[rows], cot_v.at[rows], cot_sem.at[layer])

    loads = [
        pltpu.make_async_copy(perm_h, perm_v, load_sem.at[1]),
        pltpu.make_async_copy(mask_h, mask_v, load_sem.at[2]),
    ]
    table_loads = [
        pltpu.make_async_copy(cells_h, cells_ref, load_sem.at[3]),
        pltpu.make_async_copy(helper_h, helper_ref, load_sem.at[4]),
    ]
    for copy in loads:
        copy.start()
    for layer in range(LAYERS):
        cot_copy(layer).start()

    barrier = pltpu.get_barrier_semaphore()

    def greet(step, carry):
        pl.semaphore_signal(
            barrier, inc=1, device_id=device(lax.rem(me + step, DEVICES)), device_id_type=MESH
        )
        return carry

    lax.fori_loop(1, DEVICES, greet, 0)

    for copy in table_loads:
        copy.start()

    def block_copy(which, layer):
        source, held = ((diag_h, diag_v), (flux_h, flux_v))[which]
        return pltpu.make_async_copy(source.at[layer], held.at[layer], blk_sem.at[which, layer])

    for which in range(2):
        for layer in range(LAYERS):
            block_copy(which, layer).start()
    flash_loads = [
        pltpu.make_async_copy(inv_h, inv_v, fl_sem.at[0]),
        pltpu.make_async_copy(coup_h, coup_v, fl_sem.at[1]),
        pltpu.make_async_copy(phase_h, phase_v, fl_sem.at[2]),
    ]
    for copy in flash_loads:
        copy.start()

    w_v[pl.ds(0, NC * PAD), :] = jnp.zeros((NC * PAD, CX), F32)
    w_v[pl.ds((FIELDS + NC) * PAD, NC * PAD), :] = jnp.zeros((NC * PAD, CX), F32)
    k_v[pl.ds(0, PAD), :] = jnp.zeros((PAD, CX), F32)
    k_v[pl.ds((LAYERS + 1) * PAD, PAD), :] = jnp.zeros((PAD, CX), F32)

    for copy in loads:
        copy.wait()

    lane_y = lax.broadcasted_iota(jnp.int32, (CY, CX), 1)
    hole = mask_v[...].astype(F32)
    keep = 1.0 - hole

    def field(q):
        return pl.ds(pl.multiple_of(q * CY, CY), CY)

    def pack_edges(q, value, carry):
        right, left = carry
        turned = pltpu.roll(value, 2 * q + 2, axis=1)
        right = jnp.where(lane_y == 2 * q + 1, turned, right)
        left = jnp.where(lane_y == 2 * q + 2, turned, left)
        return right, left

    def mask_fields(source, which, start):
        def step(layer, carry):
            if which == 0:
                cot_copy(layer).wait()
            for c in range(NC):
                q = layer * NC + c
                value = source[field(q), :] * keep
                w_v[pl.ds(pl.multiple_of((q + NC) * PAD + 8, 8), CY), :] = value
                carry = pack_edges(q, value, carry)
            return carry

        right, left = lax.fori_loop(0, LAYERS, step, start)
        hx_s[which, 0] = pltpu.roll(left, CX - 2, axis=1)
        hx_s[which, 1] = right
        for layer in range(LAYERS):
            base = (layer + 1) * NC * PAD + 8
            hy_s[which, 0, pl.ds(layer * NC, NC), :] = w_v[pl.ds(base, NC, stride=PAD), :]
            hy_s[which, 1, pl.ds(layer * NC, NC), :] = w_v[pl.ds(base + CY - 1, NC, stride=PAD), :]

    def halo_copies(which):
        east = (lax.rem(gx + 1, WX), gy)
        west = (lax.rem(gx + WX - 1, WX), gy)
        south = (gx, lax.rem(gy + 1, WY))
        north = (gx, lax.rem(gy + WY - 1, WY))
        plan = (
            (hx_s.at[which, 1], hx_r.at[which, 0], east),
            (hx_s.at[which, 0], hx_r.at[which, 1], west),
            (hy_s.at[which, 1], hy_r.at[which, 0], south),
            (hy_s.at[which, 0], hy_r.at[which, 1], north),
        )
        return [
            pltpu.make_async_remote_copy(
                src_ref=source,
                dst_ref=target_ref,
                send_sem=halo_send.at[which, i],
                recv_sem=halo_recv.at[which, i],
                device_id=where,
                device_id_type=MESH,
            )
            for i, (source, target_ref, where) in enumerate(plan)
        ]

    def edge_columns(which):
        odd = lax.rem(lane_y, 2) == 1
        from_west = jnp.where(gx > 0, hx_r[which, 0], 0.0)
        from_east = jnp.where(gx < WX - 1, hx_r[which, 1], 0.0)
        hx_r[which, 0] = jnp.where(odd, from_west, from_east)

    def edge_rows(which):
        for layer in range(LAYERS):
            base = (layer + 1) * NC * PAD
            rows = pl.ds(layer * NC, NC)
            w_v[pl.ds(base + 7, NC, stride=PAD), :] = jnp.where(gy > 0, hy_r[which, 0, rows, :], 0.0)
            w_v[pl.ds(base + 8 + CY, NC, stride=PAD), :] = jnp.where(
                gy < WY - 1, hy_r[which, 1, rows, :], 0.0
            )

    zero_edge = jnp.zeros((CY, CX), F32)
    start = (zero_edge, zero_edge)
    for layer in range(LAYERS):
        value = perm_v[pl.ds(layer * CY, CY), :]
        k_v[pl.ds((layer + 1) * PAD + 8, CY), :] = value
        start = pack_edges(FIELDS + layer, value, start)
    mask_fields(cot_v, 0, start)
    for layer in range(LAYERS):
        base = (layer + 1) * PAD + 8
        hy_s[0, 0, pl.ds(FIELDS + layer, 1), :] = k_v[pl.ds(base, 1), :]
        hy_s[0, 1, pl.ds(FIELDS + layer, 1), :] = k_v[pl.ds(base + CY - 1, 1), :]

    pl.semaphore_wait(barrier, DEVICES - 1)
    first_halo = halo_copies(0)
    for copy in first_halo:
        copy.start()

    def beside_x(edges, q, lane, west, east):
        turned = pltpu.roll(edges, CX - 1 - 2 * q, axis=1)
        return jnp.where(lane == 0, turned, west), jnp.where(lane == CX - 1, turned, east)

    def make_weights(layer, carry):
        base = pl.multiple_of((layer + 1) * PAD, 8)
        centre = k_v[pl.ds(base + 8, CY), :]
        west, east = beside_x(
            hx_r[0, 0],
            FIELDS + layer,
            lane_y,
            pltpu.roll(centre, 1, axis=1),
            pltpu.roll(centre, CX - 1, axis=1),
        )
        others = (
            k_v[pl.ds(base + 8 + PAD, CY), :],
            k_v[pl.ds(base + 8 - PAD, CY), :],
            k_v[pl.ds(base + 9, CY), :],
            k_v[pl.ds(base + 7, CY), :],
            east,
            west,
        )
        for i, other in enumerate(others):
            t_v[i, field(layer), :] = 2.0 * centre * other / (centre + other)
        return carry

    lane_r = lax.broadcasted_iota(jnp.int32, (ROWS, CX), 1)

    def part_rows(layer, c, r0):
        return pl.ds(pl.multiple_of((layer * NC + c) * CY + r0, ROWS), ROWS)

    def diag_pass(layer, source, held):
        for r0 in range(0, CY, ROWS):
            well = mask_v[pl.ds(r0, ROWS), :].astype(F32)
            acc = [well * source[part_rows(layer, c, r0), :] for c in range(NC)]
            for r in range(NC):
                base = pl.multiple_of((layer + 1) * (NC * PAD) + (r * PAD + 8 + r0), 8)
                own = w_v[pl.ds(base, ROWS), :]
                west_v[part_rows(layer, r, r0), :] = pltpu.roll(own, 1, axis=1)
                east_v[part_rows(layer, r, r0), :] = pltpu.roll(own, CX - 1, axis=1)
                for c in range(NC):
                    acc[c] = acc[c] + diag_v[layer, r, c, pl.ds(r0, ROWS), :].astype(F32) * own
            for c in range(NC):
                held[part_rows(layer, c, r0), :] = acc[c]

    def flux_pass(layer, which, held, put):
        for r0 in range(0, CY, ROWS):
            rows = pl.ds(pl.multiple_of(layer * CY + r0, ROWS), ROWS)
            weights = [t_v[i, rows, :] for i in range(6)]
            edges = hx_r[which, 0, pl.ds(r0, ROWS), :]
            acc = [held[part_rows(layer, c, r0), :] for c in range(NC)]
            for r in range(NC):
                base = pl.multiple_of((layer + 1) * (NC * PAD) + (r * PAD + 8 + r0), 8)
                here = part_rows(layer, r, r0)
                west, east = beside_x(
                    edges, layer * NC + r, lane_r, west_v[here, :], east_v[here, :]
                )
                total = weights[0] * w_v[pl.ds(base + NC * PAD, ROWS), :]
                total = total + weights[1] * w_v[pl.ds(base - NC * PAD, ROWS), :]
                total = total + weights[2] * w_v[pl.ds(base + 1, ROWS), :]
                total = total + weights[3] * w_v[pl.ds(base - 1, ROWS), :]
                total = total + weights[4] * east
                total = total + weights[5] * west
                for c in range(NC):
                    acc[c] = acc[c] - flux_v[layer, r, c, pl.ds(r0, ROWS), :].astype(F32) * total
            for c in range(NC):
                put(layer, c, r0, acc[c])

    def put_first(layer, c, r0, value):
        lanes = pl.ds(pl.multiple_of(layer * CX, CX), CX)
        f16_v[pl.ds(c * CY + r0, ROWS), lanes] = value.astype(BF16)
        s2_v[part_rows(layer, c, r0), :] = value

    def first_diag(layer, carry):
        block_copy(0, layer).wait()
        diag_pass(layer, cot_v, s2_v)
        return carry

    def first_flux(layer, carry):
        block_copy(1, layer).wait()
        flux_pass(layer, 0, s2_v, put_first)
        return carry

    lax.fori_loop(0, LAYERS, first_diag, 0)

    for copy in table_loads:
        copy.wait()
    lane_i = lax.broadcasted_iota(jnp.int32, (BLOCKS, BLK), 1)
    row_i = lax.broadcasted_iota(jnp.int32, (BLOCKS, BLK), 0)
    target = lax.rem(row_i + me + 1, DEVICES)
    choose = jnp.where(helper_ref[...] == target, 1.0, 0.0).astype(BF16)
    cells = cells_ref[...]
    cell_layer = lax.shift_right_logical(cells, 13).astype(F32).astype(BF16)
    cell_y = lax.shift_right_logical(cells, 7) & (CY - 1)
    cell_y = jnp.where(row_i < count_ref[0, 0], cell_y, CY).astype(F32).astype(BF16)
    cell_x = (cells & (CX - 1)).astype(F32).astype(BF16)
    code_v[...] = CX * jnp.dot(choose, cell_layer, preferred_element_type=F32) + jnp.dot(
        choose, cell_x, preferred_element_type=F32
    )
    y_v[...] = jnp.dot(choose, cell_y, preferred_element_type=F32)

    for copy in first_halo:
        copy.wait_recv()
    edge_columns(0)
    edge_rows(0)
    for layer in range(LAYERS):
        base = (layer + 1) * PAD
        k_v[pl.ds(base + 7, 1), :] = jnp.where(gy > 0, hy_r[0, 0, pl.ds(FIELDS + layer, 1), :], 0.0)
        k_v[pl.ds(base + 8 + CY, 1), :] = jnp.where(
            gy < WY - 1, hy_r[0, 1, pl.ds(FIELDS + layer, 1), :], 0.0
        )
    lax.fori_loop(0, LAYERS, make_weights, 0)
    lax.fori_loop(0, LAYERS, first_flux, 0)
    for copy in flash_loads:
        copy.wait()

    iota_x = lax.broadcasted_iota(jnp.int32, (CX, BLK), 0).astype(F32).astype(BF16)
    iota_y = lax.broadcasted_iota(jnp.int32, (CY, BLK), 0).astype(F32)
    iota_y16 = iota_y.astype(BF16)
    one16 = jnp.ones((CX, BLK), BF16)
    zero16 = jnp.zeros((CX, BLK), BF16)

    def one_hot(chunk, b):
        code = code_v[pl.ds(chunk * NB + b, 1), :]
        for layer in range(LAYERS):
            own_x = jnp.broadcast_to((code - float(layer * CX)).astype(BF16), (CX, BLK))
            oh_v[chunk, b, pl.ds(layer * CX, CX), :] = jnp.where(
                own_x == iota_x, one16, zero16
            )

    def send_chunk(buf, to, chunk, sign, send, recv):
        for b in range(NB):
            p = chunk * NB + b

            def remote():
                pltpu.make_async_remote_copy(
                    src_ref=buf.at[p],
                    dst_ref=to.at[p],
                    send_sem=send.at[chunk],
                    recv_sem=recv.at[chunk],
                    device_id=device(lax.rem(me + sign * (p + 1) + DEVICES, DEVICES)),
                    device_id_type=MESH,
                ).start()

            if b < NB - 1:
                remote()
            else:
                pl.when(chunk < CHUNKS - 1)(remote)

                @pl.when(chunk == CHUNKS - 1)
                def _():
                    pltpu.make_async_copy(buf.at[p], to.at[p], recv.at[chunk]).start()

    def chunk_copy(buf, to, chunk, count, send, recv):
        rows = pl.ds(chunk * NB, count)
        return pltpu.make_async_remote_copy(
            src_ref=buf.at[rows],
            dst_ref=to.at[rows],
            send_sem=send.at[chunk],
            recv_sem=recv.at[chunk],
            device_id=device(lax.rem(me + 1, DEVICES)),
            device_id_type=MESH,
        )

    def gather(chunk):
        for first in range(0, NB, SUB):
            for b in range(first, first + SUB):
                one_hot(chunk, b)
            wide = jnp.dot(
                f16_v[...],
                jnp.concatenate([oh_v[chunk, first + b] for b in range(SUB)], axis=1),
                preferred_element_type=F32,
            )
            for b in range(SUB):
                p = chunk * NB + first + b
                hit = jnp.broadcast_to(y_v[pl.ds(p, 1), :], (CY, BLK)) == iota_y
                found = []
                for c in range(NC):
                    piece = wide[c * CY : (c + 1) * CY, b * BLK : (b + 1) * BLK]
                    found.append(jnp.sum(jnp.where(hit, piece, 0.0), axis=0, keepdims=True))
                ps[p] = jnp.concatenate(found, axis=0).astype(BF16)

    def spread(value, b, i):
        row_v[b, i] = value
        return [jnp.broadcast_to(row_v[b, i, pl.ds(r, 1), :], (NC, BLK)) for r in range(NC)]

    def weighted(matrix, rows):
        total = matrix[0] * rows[0]
        for r in range(1, NC):
            total = total + matrix[r] * rows[r]
        return total

    def flash(chunk):
        totals = [g_v[j] for j in range(NC)]
        for b in range(NB):
            p = chunk * NB + b
            source = lax.rem(me - (p + 1) + DEVICES, DEVICES)
            multiplier = weighted(inv_v[source].astype(F32), spread(rb[p].astype(F32), b, 0))
            change = -weighted(coup_v[source].astype(F32), spread(multiplier, b, 1))
            cs[p] = change.astype(BF16)
            state = phase_v[source].astype(F32)
            term = multiplier * state
            for j, row in enumerate(spread(state, b, 2)):
                totals[j] = totals[j] + term * row
        for j in range(NC):
            g_v[j] = totals[j]

    def scatter(chunk):
        for b in range(NB):
            p = chunk * NB + b
            hit = jnp.broadcast_to(y_v[pl.ds(p, 1), :].astype(BF16), (CY, BLK)) == iota_y16
            change = cr[p]
            for c in range(NC):
                lhs_v[b, pl.ds(c * CY, CY), :] = jnp.where(
                    hit, jnp.broadcast_to(change[c : c + 1], (CY, BLK)), zero16[:CY]
                )
        added = lax.dot_general(
            jnp.concatenate([lhs_v[b] for b in range(NB)], axis=1),
            jnp.concatenate([oh_v[chunk, b] for b in range(NB)], axis=1),
            (((1,), (1,)), ((), ())),
            preferred_element_type=F32,
        )
        for layer in range(LAYERS):
            rows = pl.ds(layer * NC * CY, NC * CY)
            s2_v[rows, :] = s2_v[rows, :] + added[:, layer * CX : (layer + 1) * CX]

    g_v[...] = jnp.zeros_like(g_v)

    def loop(low, high, gathers=None, flashes=None, scatters=None):
        def body(t, carry):
            if flashes is not None:
                chunk_copy(ps, rb, t - flashes, NB, ps_send, ps_recv).wait_recv()
            if scatters is not None:
                chunk_copy(cs, cr, t - scatters, NB, cs_send, cs_recv).wait_recv()
            if gathers is not None:
                gather(t - gathers)
            if flashes is not None:
                flash(t - flashes)
            if scatters is not None:
                scatter(t - scatters)
            if gathers is not None:
                send_chunk(ps, rb, t - gathers, 1, ps_send, ps_recv)
            if flashes is not None:
                send_chunk(cs, cr, t - flashes, -1, cs_send, cs_recv)
            return carry

        lax.fori_loop(low, high, body, 0)

    loop(0, DELAY, gathers=0)
    loop(DELAY, CHUNKS, gathers=0, flashes=DELAY)
    loop(CHUNKS, CHUNKS + DELAY, flashes=DELAY, scatters=CHUNKS)

    lane_g = lax.broadcasted_iota(jnp.int32, (NC, CX), 1)
    tile = jnp.zeros((NC, CX), F32)
    for j in range(NC):
        tile = jnp.where(lane_g == j, jnp.sum(g_v[j], axis=1, keepdims=True), tile)
    gt[...] = tile
    ga[gx] = tile

    def grad_copy(source, target_ref, where, phase):
        return pltpu.make_async_remote_copy(
            src_ref=source,
            dst_ref=target_ref,
            send_sem=g_send.at[phase],
            recv_sem=g_recv.at[phase],
            device_id=where,
            device_id_type=MESH,
        )

    def send_x(step, carry):
        grad_copy(gt, ga.at[gx], (lax.rem(gx + step, WX), gy), 0).start()
        return carry

    lax.fori_loop(1, WX, send_x, 0)

    loop(CHUNKS + DELAY, 2 * CHUNKS, scatters=CHUNKS)

    mask_fields(s2_v, 1, (zero_edge, zero_edge))
    second_halo = halo_copies(1)
    for copy in second_halo:
        copy.start()

    some = ga.at[pl.ds(0, WX - 1)]
    grad_copy(some, some, (lax.rem(gx + 1, WX), gy), 0).wait_recv()
    part = ga[0]
    for i in range(1, WX):
        part = part + ga[i]
    gt2[...] = part
    gb[gy] = part

    def send_y(step, carry):
        grad_copy(gt2, gb.at[gy], (gx, lax.rem(gy + step, WY)), 1).start()
        return carry

    lax.fori_loop(1, WY, send_y, 0)


    def second_diag(layer, carry):
        diag_pass(layer, s2_v, out_v)
        return carry

    lax.fori_loop(0, LAYERS, second_diag, 0)
    for copy in second_halo:
        copy.wait_recv()
    edge_columns(1)
    edge_rows(1)

    def put_second(layer, c, r0, value):
        out_v[part_rows(layer, c, r0), :] = value

    def second_flux(layer, carry):
        flux_pass(layer, 1, out_v, put_second)
        return carry

    lax.fori_loop(0, LAYERS, second_flux, 0)

    some = gb.at[pl.ds(0, WY - 1)]
    grad_copy(some, some, (gx, lax.rem(gy + 1, WY)), 1).wait_recv()
    total = gb[0]
    for i in range(1, WY):
        total = total + gb[i]
    scale = -1.0 / math.sqrt(BLK * BLOCKS * DEVICES)
    grad_ref[...] = scale * total[:, :NC]

    for copy in first_halo + second_halo:
        copy.wait_send()
    some = ga.at[pl.ds(0, WX - 1)]
    grad_copy(some, some, (lax.rem(gx + 1, WX), gy), 0).wait_send()
    some = gb.at[pl.ds(0, WY - 1)]
    grad_copy(some, some, (gx, lax.rem(gy + 1, WY)), 1).wait_send()

    def drain(chunk, carry):
        chunk_copy(ps, rb, chunk, NB, ps_send, ps_recv).wait_send()
        chunk_copy(cs, cr, chunk, NB, cs_send, cs_recv).wait_send()
        return carry

    lax.fori_loop(0, CHUNKS - 1, drain, 0)
    chunk_copy(ps, rb, CHUNKS - 1, NB - 1, ps_send, ps_recv).wait_send()
    chunk_copy(cs, cr, CHUNKS - 1, NB - 1, cs_send, cs_recv).wait_send()


def shards(
    cotangent, permeability, well_mask, diag_block, flux_block, cell_list, block_count, helper_of,
    flash_inverse, flash_coupling, phase_state,
):
    hbm = pl.BlockSpec(memory_space=pltpu.HBM)
    smem = pl.BlockSpec(memory_space=pltpu.SMEM)
    vmem = pl.BlockSpec(memory_space=pltpu.VMEM)
    dma = pltpu.SemaphoreType.DMA
    def pin(array):
        return pltpu.with_memory_space_constraint(array, pltpu.HBM)

    adjoint, grad = pl.pallas_call(
        kernel,
        out_shape=(
            pltpu.VMEM((FIELDS * CY, CX), F32),
            pltpu.VMEM((NC, NC), F32),
        ),
        in_specs=[hbm] * 6 + [smem] + [hbm] * 4,
        out_specs=(vmem, vmem),
        scratch_shapes=[
            pltpu.VMEM((FIELDS * CY, CX), F32),
            pltpu.VMEM((LAYERS * CY, CX), F32),
            pltpu.VMEM((CY, CX), jnp.int32),
            pltpu.VMEM((BLOCKS, BLK), jnp.int32),
            pltpu.VMEM((1, BLOCKS), jnp.int32),
            pltpu.VMEM((LAYERS, NC, NC, CY, CX), BF16),
            pltpu.VMEM((LAYERS, NC, NC, CY, CX), BF16),
            pltpu.VMEM((BLOCKS, NC, NC, BLK), BF16),
            pltpu.VMEM((BLOCKS, NC, NC, BLK), BF16),
            pltpu.VMEM((BLOCKS, NC, BLK), BF16),
            pltpu.VMEM(((FIELDS + 2 * NC) * PAD, CX), F32),
            pltpu.VMEM((FIELDS * CY, CX), F32),
            pltpu.VMEM((FIELDS * CY, CX), F32),
            pltpu.VMEM(((LAYERS + 2) * PAD, CX), F32),
            pltpu.VMEM((6, LAYERS * CY, CX), F32),
            pltpu.VMEM((NC * CY, LAYERS * CX), BF16),
            pltpu.VMEM((FIELDS * CY, CX), F32),
            pltpu.VMEM((BLOCKS, BLK), F32),
            pltpu.VMEM((BLOCKS, BLK), F32),
            pltpu.VMEM((CHUNKS, NB, LAYERS * CX, BLK), BF16),
            pltpu.VMEM((NB, NC * CY, BLK), BF16),
            pltpu.VMEM((BLOCKS, NC, BLK), BF16),
            pltpu.VMEM((BLOCKS, NC, BLK), BF16),
            pltpu.VMEM((BLOCKS, NC, BLK), BF16),
            pltpu.VMEM((BLOCKS, NC, BLK), BF16),
            pltpu.VMEM((NB, 3, NC, BLK), F32),
            pltpu.VMEM((NC, NC, BLK), F32),
            pltpu.VMEM((NC, CX), F32),
            pltpu.VMEM((WX, NC, CX), F32),
            pltpu.VMEM((NC, CX), F32),
            pltpu.VMEM((WY, NC, CX), F32),
            pltpu.VMEM((2, 2, CY, CX), F32),
            pltpu.VMEM((2, 2, CY, CX), F32),
            pltpu.VMEM((2, 2, 56, CX), F32),
            pltpu.VMEM((2, 2, 56, CX), F32),
            dma((5,)),
            dma((LAYERS,)),
            dma((2, LAYERS)),
            dma((3,)),
            dma((2, 4)),
            dma((2, 4)),
            dma((CHUNKS,)),
            dma((CHUNKS,)),
            dma((CHUNKS,)),
            dma((CHUNKS,)),
            dma((2,)),
            dma((2,)),
        ],
        compiler_params=pltpu.CompilerParams(
            collective_id=0, has_side_effects=True, vmem_limit_bytes=60 << 20
        ),
    )(
        pin(cotangent.reshape(FIELDS * CY, CX)),
        pin(permeability.reshape(LAYERS * CY, CX)),
        pin(well_mask),
        pin(diag_block),
        pin(flux_block),
        pin(cell_list.reshape(BLOCKS, BLK)),
        block_count,
        pin(helper_of.reshape(1, BLOCKS)),
        pin(flash_inverse.reshape(BLOCKS, NC, NC, BLK)),
        pin(flash_coupling.reshape(BLOCKS, NC, NC, BLK)),
        pin(phase_state.reshape(BLOCKS, NC, BLK)),
    )
    return adjoint.reshape(cotangent.shape), grad


def solution(mesh):
    return jax.shard_map(
        shards,
        mesh=mesh,
        in_specs=(
            P(None, None, "gy", "gx"),
            P(None, "gy", "gx"),
            P("gy", "gx"),
            P(None, None, None, "gy", "gx"),
            P(None, None, None, "gy", "gx"),
            P("gy", "gx", None),
            P("gy", "gx"),
            P("gy", "gx", None),
            P("gy", "gx", None, None, None, None),
            P("gy", "gx", None, None, None, None),
            P("gy", "gx", None, None, None),
        ),
        out_specs=(P(None, None, "gy", "gx"), P()),
        check_vma=False,
    )
```
